32 devices in a mesh: group: 2 (over x), row: 16 (over z, y, core).
Axes of the slice: x: 2, y: 2, z: 4, core: 2. Of those that a mesh axis runs over, the one named last changes fastest.
Arguments:
- one_input: bfloat16 [16, 512, 256], P('group', 'row'), parts along dimension 0, may hold values from -6 to 6
- pair_input: bfloat16 [16, 512, 32, 512], P('group', 'row'), parts along dimension 0, may hold values from -6 to 6
- spins: int32 [16, 512], P('group'), parts along dimension 0, may hold values from 0 to 1, as said below
- cotangent: float32 [16, 512, 256], P('group', 'row'), parts along dimension 0, may hold values from -0.09375 to 0.09375
- w_self: bfloat16 [3, 256, 256], replicated, may hold values from -0.375 to 0.375
- w_means: bfloat16 [3, 512, 256], replicated, may hold values from -4 to 4
- w_rows: bfloat16 [3, 64, 256], replicated, may hold values from -6 to 6
- w_cols: bfloat16 [3, 64, 256], replicated, may hold values from -6 to 6
- b_one: float32 [3, 256], replicated, may hold values from -3 to 3
- w_pair: bfloat16 [2, 32, 32], replicated, may hold values from -1 to 1
- b_pair: float32 [2, 32], replicated, may hold values from -2 to 2
Outputs:
- one_output: bfloat16 [16, 512, 256], P('group', 'row'), parts along dimension 0
- grad_self: float32 [6, 256, 256], P('group'), parts along dimension 0
- grad_means: float32 [6, 512, 256], P('group'), parts along dimension 0
- grad_rows: float32 [6, 64, 256], P('group'), parts along dimension 0
- grad_cols: float32 [6, 64, 256], P('group'), parts along dimension 0
- grad_bias: float32 [6, 256], P('group'), parts along dimension 0
- grad_wpair: float32 [4, 32, 32], P('group'), parts along dimension 0
- grad_bpair: float32 [4, 32], P('group'), parts along dimension 0
The draws below stay inside these ranges and needn't reach their ends.
There are 2 independent parts, one for each index of `group`. The reference program is written for one: setup_inputs(seed, part) draws one part's arguments, and reference() takes and returns one part's arrays. A program takes and returns all parts, laid end to end along the dimension named above; an argument that names none is the same for every part. Nothing has to cross between parts.
Inputs may be any that keep to these rules, and one draw needn't show every extreme that they name: `spins`: every walker has at least 128 electrons of each spin; in every draw some walker has exactly 128 up electrons and another exactly 128 down electrons.
All inputs are finite; a program needn't handle non-finite values.
Results may differ from the reference program's by a relative error of at most 0.009.
The reference program's roundings to bfloat16 on the way count: a program that leaves them out, or rounds other values in their place, can miss the bound.
Values sent between devices are 32-bit elements; how exact they have to be, the bound alone decides.
A program may use at most 192 MiB of HBM per device.

```python
import jax
import jax.numpy as jnp
from jax import lax

ELECTRONS = 512
ONE_WIDTH = 256
PAIR_WIDTH = 32
LAYERS = 3
WALKERS = 8


def walker_order(one_key):
    return jax.random.permutation(one_key, ELECTRONS)


def draw_spins(key, part):
    key_count, key_order, key_chosen = jax.random.split(jax.random.fold_in(key, 17), 3)
    up_counts = jax.random.randint(key_count, (WALKERS,), ELECTRONS // 4, ELECTRONS - ELECTRONS // 4 + 1)
    chosen = jax.random.randint(key_chosen, (), 0, WALKERS)
    other = (chosen + 1) % WALKERS
    walker_ids = jnp.arange(WALKERS)
    up_counts = jnp.where(walker_ids == chosen, ELECTRONS // 4, up_counts)
    up_counts = jnp.where(walker_ids == other, ELECTRONS - ELECTRONS // 4, up_counts)
    walker_keys = jax.random.split(key_order, WALKERS)
    ranking = jax.vmap(walker_order)(walker_keys)
    return (ranking < up_counts[:, None]).astype(jnp.int32)


def block_levels(rng, dims, shards, least, top_value):
    level = 1.0
    for axis_at, blocks in shards:
        steps = jax.random.uniform(jax.random.fold_in(jax.random.fold_in(rng, 6), axis_at), (blocks,), jnp.float32, least / len(shards), top_value / len(shards))
        level = level * jnp.repeat(jnp.exp(steps), dims[axis_at] // blocks).reshape((-1,) + (1,) * (len(dims) - 1 - axis_at))
    return level


def noise(key, extent, spread, limit, shards=(), kind=jnp.bfloat16):
    gain = block_levels(key, extent, shards, -0.22, 0.18) if shards else 1.0
    entries = jax.random.normal(key, extent, jnp.float32) * spread * gain
    return jnp.minimum(jnp.maximum(entries, -limit), limit).astype(kind)


def setup_inputs(seed: int = 0, part: int = 0) -> dict:
    splits = jax.random.split(jax.random.key(seed), 12)
    own_keys = jax.random.split(jax.random.fold_in(splits[11], part), 12)
    one_input = noise(own_keys[0], (WALKERS, ELECTRONS, ONE_WIDTH), 1.0, 6.0, ((1, 16),))
    pair_input = noise(own_keys[1], (WALKERS, ELECTRONS, PAIR_WIDTH, ELECTRONS), 1.0, 6.0, ((1, 16),))
    spins = draw_spins(jax.random.fold_in(jax.random.fold_in(splits[11], part), 71), part)
    cotangent = noise(own_keys[3], (WALKERS, ELECTRONS, ONE_WIDTH), (WALKERS * ELECTRONS) ** -0.5, 0.09375, ((1, 16),), jnp.float32)
    w_self = noise(splits[4], (LAYERS, ONE_WIDTH, ONE_WIDTH), ONE_WIDTH ** -0.5, 0.375)
    w_means = noise(splits[5], (LAYERS, 2 * ONE_WIDTH, ONE_WIDTH), 0.25, 4.0)
    w_rows = noise(splits[6], (LAYERS, 2 * PAIR_WIDTH, ONE_WIDTH), 1.0, 6.0)
    w_cols = noise(splits[7], (LAYERS, 2 * PAIR_WIDTH, ONE_WIDTH), 1.0, 6.0)
    b_one = noise(splits[8], (LAYERS, ONE_WIDTH), 0.5, 3.0, (), jnp.float32)
    w_pair = noise(splits[9], (LAYERS - 1, PAIR_WIDTH, PAIR_WIDTH), PAIR_WIDTH ** -0.5, 1.0)
    b_pair = noise(splits[10], (LAYERS - 1, PAIR_WIDTH), 0.3, 2.0, (), jnp.float32)
    return {"one_input": one_input, "pair_input": pair_input, "spins": spins, "cotangent": cotangent, "w_self": w_self, "w_means": w_means, "w_rows": w_rows, "w_cols": w_cols, "b_one": b_one, "w_pair": w_pair, "b_pair": b_pair}


def pair_tanh(pair_wide, weight, bias):
    zvals = jnp.einsum('wicj,cd->widj', pair_wide, weight.astype(jnp.float32), precision=lax.Precision.HIGHEST)
    return jnp.tanh(zvals + bias[None, None, :, None])


def reference(one_input, pair_input, spins, cotangent, w_self, w_means, w_rows, w_cols, b_one, w_pair, b_pair):
    highest = lax.Precision.HIGHEST
    walkers, electrons, one_width = one_input.shape
    pair_width = pair_input.shape[2]
    up_mask = (spins == 1).astype(jnp.float32)
    spin_mask = jnp.stack([up_mask, 1.0 - up_mask], axis=2)
    counts = jnp.sum(spin_mask, axis=1)
    one_cur = one_input
    pair_cur = pair_input
    stored = []
    for layer_index in range(LAYERS):
        one_sums = jnp.einsum('wjs,wjh->wsh', spin_mask, one_cur.astype(jnp.float32), precision=highest)
        one_means = (one_sums / counts[:, :, None]).astype(jnp.bfloat16).reshape(walkers, 2 * one_width)
        pair_wide = pair_cur.astype(jnp.float32)
        row_sums = jnp.einsum('wicj,wjs->wisc', pair_wide, spin_mask, precision=highest)
        row_means = (row_sums / counts[:, None, :, None]).astype(jnp.bfloat16).reshape(walkers, electrons, 2 * pair_width)
        col_sums = jnp.einsum('wicj,wis->wjsc', pair_wide, spin_mask, precision=highest)
        col_means = (col_sums / counts[:, None, :, None]).astype(jnp.bfloat16).reshape(walkers, electrons, 2 * pair_width)
        preact = jnp.dot(one_cur, w_self[layer_index], preferred_element_type=jnp.float32)
        preact = preact + jnp.dot(one_means, w_means[layer_index], preferred_element_type=jnp.float32)[:, None, :]
        preact = preact + jnp.dot(row_means, w_rows[layer_index], preferred_element_type=jnp.float32)
        preact = preact + jnp.dot(col_means, w_cols[layer_index], preferred_element_type=jnp.float32)
        preact = preact + b_one[layer_index]
        activation = jnp.tanh(preact)
        stored.append((one_cur, pair_cur, one_means, row_means, col_means, activation))
        one_next = (activation + one_cur.astype(jnp.float32)).astype(jnp.bfloat16)
        if layer_index < LAYERS - 1:
            pair_cur = (pair_tanh(pair_wide, w_pair[layer_index], b_pair[layer_index]) + pair_wide).astype(jnp.bfloat16)
        one_cur = one_next
    one_output = one_cur

    grad_one = cotangent
    grad_pair = jnp.zeros((1,), jnp.float32)
    results = {}
    for layer_index in reversed(range(LAYERS)):
        one_prev, pair_prev, one_means, row_means, col_means, activation = stored[layer_index]
        grad_pre = (grad_one * (1.0 - activation * activation)).astype(jnp.bfloat16)
        flat_pre = grad_pre.reshape(-1, one_width)
        g_self = jnp.dot(one_prev.reshape(-1, one_width).T, flat_pre, preferred_element_type=jnp.float32)
        pre_sums = jnp.sum(grad_pre.astype(jnp.float32), axis=1)
        g_means = jnp.einsum('wa,wk->ak', one_means.astype(jnp.float32), pre_sums, precision=highest)
        g_rows = jnp.dot(row_means.reshape(-1, 2 * pair_width).T, flat_pre, preferred_element_type=jnp.float32)
        g_cols = jnp.dot(col_means.reshape(-1, 2 * pair_width).T, flat_pre, preferred_element_type=jnp.float32)
        g_bias = jnp.sum(flat_pre.astype(jnp.float32), axis=0)
        results[layer_index] = [g_self, g_means, g_rows, g_cols, g_bias]
        pair_wide = pair_prev.astype(jnp.float32)
        if layer_index < LAYERS - 1:
            tanh_pair = pair_tanh(pair_wide, w_pair[layer_index], b_pair[layer_index])
            grad_z = (grad_pair * (1.0 - tanh_pair * tanh_pair)).astype(jnp.bfloat16)
            grad_wide = grad_z.astype(jnp.float32)
            g_wpair = jnp.einsum('wicj,widj->cd', pair_wide, grad_wide, precision=highest)
            g_bpair = jnp.sum(grad_wide, axis=(0, 1, 3))
            results[layer_index] = results[layer_index] + [g_wpair, g_bpair]
        if layer_index > 0:
            grad_feat = jnp.einsum('weh,kh->wek', grad_pre.astype(jnp.float32), w_self[layer_index].astype(jnp.float32), precision=highest)
            mean_part = jnp.einsum('weh,ah->wa', grad_pre.astype(jnp.float32), w_means[layer_index].astype(jnp.float32), precision=highest)
            mean_total = mean_part.reshape(walkers, 2, one_width) / counts[:, :, None]
            grad_one = grad_one + grad_feat + jnp.einsum('wjs,wsh->wjh', spin_mask, mean_total, precision=highest)
            row_grad = jnp.einsum('weh,ah->wea', grad_pre.astype(jnp.float32), w_rows[layer_index].astype(jnp.float32), precision=highest)
            row_grad = row_grad.reshape(walkers, electrons, 2, pair_width) / counts[:, None, :, None]
            col_grad = jnp.einsum('weh,ah->wea', grad_pre.astype(jnp.float32), w_cols[layer_index].astype(jnp.float32), precision=highest)
            col_grad = col_grad.reshape(walkers, electrons, 2, pair_width) / counts[:, None, :, None]
            grad_mean = jnp.einsum('wisc,wjs->wicj', row_grad, spin_mask, precision=highest)
            grad_mean = grad_mean + jnp.einsum('wjsc,wis->wicj', col_grad, spin_mask, precision=highest)
            if layer_index == LAYERS - 1:
                grad_pair = grad_mean
            else:
                back_term = jnp.einsum('widj,cd->wicj', grad_wide, w_pair[layer_index].astype(jnp.float32), precision=highest)
                grad_pair = grad_pair + back_term + grad_mean
    grad_self = jnp.stack([results[k][0] for k in range(LAYERS)])
    grad_means = jnp.stack([results[k][1] for k in range(LAYERS)])
    grad_rows = jnp.stack([results[k][2] for k in range(LAYERS)])
    grad_cols = jnp.stack([results[k][3] for k in range(LAYERS)])
    grad_bias = jnp.stack([results[k][4] for k in range(LAYERS)])
    grad_wpair = jnp.stack([results[k][5] for k in range(LAYERS - 1)])
    grad_bpair = jnp.stack([results[k][6] for k in range(LAYERS - 1)])
    return (one_output, grad_self, grad_means, grad_rows, grad_cols, grad_bias, grad_wpair, grad_bpair)
```

```python
import functools
import math

import jax
import jax.numpy as jnp
from jax import lax
from jax.experimental import pallas as pl
from jax.experimental.pallas import tpu as pltpu
from jax.sharding import PartitionSpec as P

F32 = jnp.float32
BF16 = jnp.bfloat16
MESH = pl.DeviceIdType.MESH
VMEM_LIMIT = 48 * 1024 * 1024


def greet(targets):
    barrier = pltpu.get_barrier_semaphore()
    for target in targets:
        pl.semaphore_signal(barrier, inc=1, device_id={"row": target}, device_id_type=MESH)
    pl.semaphore_wait(barrier, len(targets))


def send(src, dst, send_sem, recv_sem, target):
    copy = pltpu.make_async_remote_copy(
        src_ref=src,
        dst_ref=dst,
        send_sem=send_sem,
        recv_sem=recv_sem,
        device_id={"row": target},
        device_id_type=MESH,
    )
    copy.start()
    return copy


def neighbours(near, far):
    me = lax.axis_index("row")
    low = lax.rem(me, near)
    high = me // near
    near_ids = [high * near + lax.rem(low + k, near) for k in range(1, near)]
    far_ids = [lax.rem(high + k, far) * near + low for k in range(1, far)]
    return low, high, near_ids, far_ids


def small_steps(near, far, x_ref, o_ref, slots, part, slots_far, sn, rn, sf, rf):
    low, high, near_ids, far_ids = neighbours(near, far)
    copies = [
        send(x_ref, slots.at[low], sn.at[k], rn.at[k], target) for k, target in enumerate(near_ids)
    ]
    slots[low] = x_ref[...]
    yield
    for copy in copies:
        copy.wait()
    total = slots[0]
    for k in range(1, near):
        total = total + slots[k]
    part[...] = total
    copies = [
        send(part, slots_far.at[high], sf.at[k], rf.at[k], target)
        for k, target in enumerate(far_ids)
    ]
    slots_far[high] = total
    yield
    for copy in copies:
        copy.wait()
    total = slots_far[0]
    for k in range(1, far):
        total = total + slots_far[k]
    o_ref[...] = total
    yield


def greet_all(near, far):
    low, high, near_ids, far_ids = neighbours(near, far)
    greet(near_ids + far_ids)


def reduce_small_kernel(near, far, *refs):
    greet_all(near, far)
    for _ in small_steps(near, far, *refs):
        pass


def small_scratch(near, far, shape):
    return [
        pltpu.VMEM((near,) + shape, F32),
        pltpu.VMEM(shape, F32),
        pltpu.VMEM((far,) + shape, F32),
        pltpu.SemaphoreType.DMA((near,)),
        pltpu.SemaphoreType.DMA((near,)),
        pltpu.SemaphoreType.DMA((far,)),
        pltpu.SemaphoreType.DMA((far,)),
    ]


def reduce_small(x, size, collective_id):
    near = math.gcd(size, 4)
    far = size // near
    return pl.pallas_call(
        functools.partial(reduce_small_kernel, near, far),
        out_shape=jax.ShapeDtypeStruct(x.shape, F32),
        in_specs=[pl.BlockSpec(memory_space=pltpu.VMEM)],
        out_specs=pl.BlockSpec(memory_space=pltpu.VMEM),
        scratch_shapes=small_scratch(near, far, x.shape),
        compiler_params=pltpu.CompilerParams(collective_id=collective_id, has_side_effects=True),
    )(x)


def position():
    me = lax.axis_index("row")
    return me, lax.rem(me, 2), lax.rem(me // 2, 2), me // 4


def scatter_steps(parts, far, x_ref, half, quarter, landed, sems, small):
    me, core, side, high = position()
    peer_core = me + 1 - 2 * core
    peer_side = me + 2 - 4 * side
    far_ids = [lax.rem(high + k, far) for k in range(1, far)]
    sa, ra, sb, rb, sc, rc = sems
    first, second, third = [], [], []
    for k in range(parts):
        first.append(send(x_ref.at[k, :, :, 1 - core], half.at[k], sa.at[k], ra.at[k], peer_core))
    next(small)
    for k in range(parts):
        first[k].wait()
        half[k] = half[k] + x_ref[k, :, :, core]
        second.append(send(half.at[k, :, 1 - side], quarter.at[k], sb.at[k], rb.at[k], peer_side))
    next(small)
    for k in range(parts):
        second[k].wait()
        quarter[k] = quarter[k] + half[k, :, side]
        third.append(
            [
                send(
                    quarter.at[k, to],
                    landed.at[k, d],
                    sc.at[k, d],
                    rc.at[k, d],
                    to * 4 + lax.rem(me, 4),
                )
                for d, to in enumerate(far_ids)
            ]
        )
    next(small)
    for k in range(parts):
        total = quarter[k, high]
        for d, copy in enumerate(third[k]):
            copy.wait()
            total = total + landed[k, d]
        yield k, total


def gather_steps(parts, far, o_ref, values, sems, small):
    me, core, side, high = position()
    peer_core = me + 1 - 2 * core
    peer_side = me + 2 - 4 * side
    far_ids = [lax.rem(high + k, far) for k in range(1, far)]
    sa, ra, sb, rb, sc, rc = sems
    first, second, third = [], [], []
    for k, value in values:
        o_ref[k, high, side, core] = value
        mine = o_ref.at[k, high, side, core]
        first.append(
            [
                send(mine, mine, sa.at[k, d], ra.at[k, d], to * 4 + lax.rem(me, 4))
                for d, to in enumerate(far_ids)
            ]
        )
    next(small)
    for k in range(parts):
        for copy in first[k]:
            copy.wait()
        block = o_ref.at[k, :, side, core]
        second.append(send(block, block, sb.at[k], rb.at[k], peer_side))
    next(small)
    for k in range(parts):
        second[k].wait()
        block = o_ref.at[k, :, :, core]
        third.append(send(block, block, sc.at[k], rc.at[k], peer_core))
    next(small)
    for k in range(parts):
        third[k].wait()


def scatter_kernel(parts, far, x_ref, y_ref, o_ref, oy_ref, *refs):
    greet_all(4, far)
    small = small_steps(4, far, y_ref, oy_ref, *refs[9:])
    for k, total in scatter_steps(parts, far, x_ref, *refs[:3], refs[3:9], small):
        o_ref[k] = total


def gather_kernel(parts, far, x_ref, y_ref, o_ref, oy_ref, *refs):
    greet_all(4, far)
    small = small_steps(4, far, y_ref, oy_ref, *refs[6:])
    gather_steps(parts, far, o_ref, [(k, x_ref[k]) for k in range(parts)], refs[:6], small)


def reduce_phase(phase, far, x_ref, o_ref, half, quarter, landed, sems):
    me = lax.axis_index("row")
    core, side, high = lax.rem(me, 2), lax.rem(me // 2, 2), me // 4
    peer_core = me + 1 - 2 * core
    peer_side = me + 2 - 4 * side
    far_ids = [(d, lax.rem(high + d + 1, far)) for d in range(far - 1)]

    def copies(which):
        def make(src, dst, slot, target):
            return pltpu.make_async_remote_copy(
                src_ref=src,
                dst_ref=dst,
                send_sem=sems[2 * which].at[slot],
                recv_sem=sems[2 * which + 1].at[slot],
                device_id={"row": target},
                device_id_type=MESH,
            )

        if which == 0:
            return [make(x_ref.at[:, :, 1 - core], half, 0, peer_core)]
        if which == 1:
            return [make(half.at[:, 1 - side], quarter, 0, peer_side)]
        if which == 2:
            return [
                make(quarter.at[to], landed.at[d], d, to * 4 + lax.rem(me, 4)) for d, to in far_ids
            ]
        if which == 3:
            mine = o_ref.at[high, side, core]
            return [make(mine, mine, d, to * 4 + lax.rem(me, 4)) for d, to in far_ids]
        if which == 4:
            return [make(o_ref.at[:, side, core], o_ref.at[:, side, core], 0, peer_side)]
        return [make(o_ref.at[:, :, core], o_ref.at[:, :, core], 0, peer_core)]

    if phase > 0:
        for copy in copies(phase - 1):
            copy.wait()
    if phase == 1:
        half[...] = half[...] + x_ref[:, :, core]
    elif phase == 2:
        quarter[...] = quarter[...] + half[:, side]
    elif phase == 3:
        total = quarter[high]
        for d, _ in far_ids:
            total = total + landed[d]
        o_ref[high, side, core] = total
    if phase < 6:
        for copy in copies(phase):
            copy.start()


def scatter_scratch(parts, far, rows, lanes):
    return [
        pltpu.VMEM((parts, far, 2, rows, lanes), F32),
        pltpu.VMEM((parts, far, rows, lanes), F32),
        pltpu.VMEM((parts, far, rows, lanes), F32),
    ]


def dma(*shapes):
    return [pltpu.SemaphoreType.DMA(shape) for shape in shapes]


def scatter_sems(parts, far):
    return dma((parts,), (parts,), (parts,), (parts,), (parts, far), (parts, far))


def gather_sems(parts, far):
    return dma((parts, far), (parts, far), (parts,), (parts,), (parts,), (parts,))


def comm_call(kernel, x, y, out_shape, scratch, collective_id):
    return pl.pallas_call(
        kernel,
        out_shape=(jax.ShapeDtypeStruct(out_shape, F32), jax.ShapeDtypeStruct(y.shape, F32)),
        in_specs=[pl.BlockSpec(memory_space=pltpu.VMEM)] * 2,
        out_specs=(pl.BlockSpec(memory_space=pltpu.VMEM),) * 2,
        scratch_shapes=scratch,
        compiler_params=pltpu.CompilerParams(
            collective_id=collective_id, has_side_effects=True, vmem_limit_bytes=VMEM_LIMIT
        ),
    )(x, y)


def reduce_scatter(x, y, size, collective_id):
    parts, _, rows, lanes = x.shape
    far = size // 4
    return comm_call(
        functools.partial(scatter_kernel, parts, far),
        x.reshape(parts, far, 2, 2, rows, lanes),
        y,
        (parts, rows, lanes),
        scatter_scratch(parts, far, rows, lanes)
        + scatter_sems(parts, far)
        + small_scratch(4, far, y.shape),
        collective_id,
    )


def all_gather(x, y, size, collective_id):
    parts, rows, lanes = x.shape
    far = size // 4
    out, total = comm_call(
        functools.partial(gather_kernel, parts, far),
        x,
        y,
        (parts, far, 2, 2, rows, lanes),
        gather_sems(parts, far) + small_scratch(4, far, y.shape),
        collective_id,
    )
    return out.reshape(parts, size, rows, lanes), total


def contract(a, b, dim_a, dim_b):
    return lax.dot_general(a, b, (((dim_a,), (dim_b,)), ((), ())), preferred_element_type=F32)


def forward_kernel(width, chunks, x_ref, mask_ref, own_ref, mix_ref, bias_ref, row_ref, col_ref):
    stream_layers = mix_ref.shape[0]
    tall = mix_ref.shape[1]
    lane = lax.broadcasted_iota(jnp.int32, (width, tall), 1)
    sub = lax.broadcasted_iota(jnp.int32, (width, tall), 0)
    eye = (lax.rem(lane, width) == sub).astype(F32)
    sums = [[], []]
    for walker in range(2):
        spin_rows = mask_ref[walker]
        cols = [None] * (stream_layers + 1)
        for chunk in range(chunks):
            here = slice(chunk * tall, (chunk + 1) * tall)
            own = own_ref[walker, :, here]
            select = jnp.concatenate([eye * own[0:1], eye * own[1:2]], axis=0).astype(BF16)
            pair = x_ref[walker, here]
            for layer in range(stream_layers + 1):
                row_ref[walker, layer, :, here] = contract(spin_rows, pair, 1, 1)[:8]
                part = contract(select, pair, 1, 0)
                cols[layer] = part if chunk == 0 else cols[layer] + part
                if layer < stream_layers:
                    zvals = contract(mix_ref[layer], pair, 1, 0)
                    bend = jnp.tanh(zvals + bias_ref[layer])
                    pair = (bend + pair.astype(F32)).astype(BF16)
        sums[walker] = cols
    for layer in range(stream_layers + 1):
        both = jnp.concatenate([sums[0][layer], sums[1][layer]], axis=0)
        col_ref[layer, 0] = both.T


def pair_forward(pair, mask_rows, own_rows, mix, bias_tall, width):
    walkers, tall_all, electrons = pair.shape
    layers = mix.shape[0] + 1
    chunks = tall_all // mix.shape[1]
    return pl.pallas_call(
        functools.partial(forward_kernel, width, chunks),
        grid=(walkers // 2,),
        out_shape=(
            jax.ShapeDtypeStruct((walkers, layers, 8, tall_all), F32),
            jax.ShapeDtypeStruct((layers, walkers // 2, electrons, 4 * width), F32),
        ),
        in_specs=[
            pl.BlockSpec((2, tall_all, electrons), lambda w: (w, 0, 0)),
            pl.BlockSpec((2,) + mask_rows.shape[1:], lambda w: (w, 0, 0)),
            pl.BlockSpec((2, 8, tall_all), lambda w: (w, 0, 0)),
            pl.BlockSpec(mix.shape, lambda w: (0, 0, 0)),
            pl.BlockSpec(bias_tall.shape, lambda w: (0, 0, 0)),
        ],
        out_specs=(
            pl.BlockSpec((2, layers, 8, tall_all), lambda w: (w, 0, 0, 0)),
            pl.BlockSpec((layers, 1, electrons, 4 * width), lambda w: (0, w, 0, 0)),
        ),
        compiler_params=pltpu.CompilerParams(vmem_limit_bytes=VMEM_LIMIT),
    )(pair, mask_rows, own_rows, mix, bias_tall)


def backward_kernel(
    width,
    chunks,
    far,
    x_steps,
    spin_ref,
    x_ref,
    mask_ref,
    row_ref,
    col_ref,
    mix_ref,
    mix_back_ref,
    bias_ref,
    feat_ref,
    gw_ref,
    gb_ref,
    sum_ref,
    turned,
    half,
    quarter,
    landed,
    gathered,
    *sems,
):
    walker = pl.program_id(0)
    slots = x_steps * chunks
    starts = [slots * share // 32 for share in (0, 2, 9, 16, 23, 30)]

    tall = mix_ref.shape[1]
    electrons = x_ref.shape[2]
    each = tall // width
    parity = lax.rem(walker, 2)

    @pl.when(walker == 0)
    def _():
        gw_ref[...] = jnp.zeros_like(gw_ref)
        gb_ref[...] = jnp.zeros_like(gb_ref)

    @pl.when(parity == 0)
    def _():
        for level in range(2):
            turned[level] = col_ref[level, 0].T.reshape(4, width, electrons)

    def grad_mean(level, chunk):
        here = slice(chunk * tall, (chunk + 1) * tall)
        row = row_ref[0, :, here]
        high = row.astype(BF16).astype(F32)
        rest = row - high
        mid = rest.astype(BF16).astype(F32)
        low = rest - mid
        split = jnp.concatenate([high, mid, low, jnp.zeros_like(row)], axis=0).astype(BF16)
        rows = contract(split, mask_ref[0, level], 0, 0)
        cols = []
        for step in range(each):
            spin = spin_ref[walker, chunk * each + step]
            cols.append(turned[level, parity * 2 + 1 - spin])
        return rows + jnp.concatenate(cols, axis=0)

    for chunk in range(chunks):
        for phase, start in enumerate(starts):
            if start % chunks == chunk:

                @pl.when(walker == start // chunks)
                def _(phase=phase):
                    if phase == 0:
                        greet_all(4, far)
                    reduce_phase(phase, far, feat_ref, gathered, half, quarter, landed, sems)

        here = slice(chunk * tall, (chunk + 1) * tall)
        pair0 = x_ref[0, here]
        bend0 = jnp.tanh(contract(mix_ref[0], pair0, 1, 0) + bias_ref[0])
        pair1 = (bend0 + pair0.astype(F32)).astype(BF16)
        bend1 = jnp.tanh(contract(mix_ref[1], pair1, 1, 0) + bias_ref[1])
        grad2 = grad_mean(1, chunk)
        gz1 = (grad2 * (1.0 - bend1 * bend1)).astype(BF16)
        gw_ref[1] += contract(pair1, gz1, 1, 1)
        wide1 = gz1.astype(F32)
        gb_ref[1] += jnp.sum(wide1.reshape(each, width, electrons), axis=0)
        grad1 = grad2 + contract(mix_back_ref[1], gz1, 1, 0) + grad_mean(0, chunk)
        gz0 = (grad1 * (1.0 - bend0 * bend0)).astype(BF16)
        gw_ref[0] += contract(pair0, gz0, 1, 1)
        gb_ref[0] += jnp.sum(gz0.astype(F32).reshape(each, width, electrons), axis=0)

    @pl.when(walker == pl.num_programs(0) - 1)
    def _():
        reduce_phase(6, far, feat_ref, gathered, half, quarter, landed, sems)
        sum_ref[...] = gathered[...]


def pair_backward(
    own_spins,
    pair,
    mask_pairs,
    row_parts,
    col_all,
    mix,
    mix_back,
    bias_tall,
    feats,
    width,
    size,
    collective_id,
):
    far = size // 4
    total, lanes = feats.shape
    padded = -(-total // (8 * size)) * 8 * size
    rows = padded // size
    shape = (far, 2, 2, rows, lanes)
    feats = jnp.pad(feats, ((0, padded - total), (0, 0))).reshape(shape)
    walkers, tall_all, electrons = pair.shape
    tall = mix.shape[1]
    gw, gb, sums = pl.pallas_call(
        functools.partial(backward_kernel, width, tall_all // tall, far, walkers),
        grid=(walkers,),
        out_shape=(
            jax.ShapeDtypeStruct((2, tall, tall), F32),
            jax.ShapeDtypeStruct((2, width, electrons), F32),
            jax.ShapeDtypeStruct(shape, F32),
        ),
        in_specs=[
            pl.BlockSpec(memory_space=pltpu.SMEM),
            pl.BlockSpec((1, tall_all, electrons), lambda w: (w, 0, 0)),
            pl.BlockSpec((1,) + mask_pairs.shape[1:], lambda w: (w, 0, 0, 0)),
            pl.BlockSpec((1, 8, tall_all), lambda w: (w, 0, 0)),
            pl.BlockSpec((2, 1, electrons, 4 * width), lambda w: (0, w // 2, 0, 0)),
            pl.BlockSpec(mix.shape, lambda w: (0, 0, 0)),
            pl.BlockSpec(mix.shape, lambda w: (0, 0, 0)),
            pl.BlockSpec(bias_tall.shape, lambda w: (0, 0, 0)),
            pl.BlockSpec(memory_space=pltpu.VMEM),
        ],
        out_specs=(
            pl.BlockSpec((2, tall, tall), lambda w: (0, 0, 0)),
            pl.BlockSpec((2, width, electrons), lambda w: (0, 0, 0)),
            pl.BlockSpec(memory_space=pltpu.VMEM),
        ),
        scratch_shapes=[
            pltpu.VMEM((2, 4, width, electrons), F32),
            pltpu.VMEM((far, 2, rows, lanes), F32),
            pltpu.VMEM((far, rows, lanes), F32),
            pltpu.VMEM((far, rows, lanes), F32),
            pltpu.VMEM(shape, F32),
        ]
        + dma((1,), (1,), (1,), (1,), (far,), (far,), (far,), (far,), (1,), (1,), (1,), (1,)),
        compiler_params=pltpu.CompilerParams(
            vmem_limit_bytes=VMEM_LIMIT, collective_id=collective_id, has_side_effects=True
        ),
    )(own_spins, pair, mask_pairs, row_parts, col_all, mix, mix_back, bias_tall, feats)
    return gw, gb, sums.reshape(padded, lanes)


def general(
    size,
    one_input,
    pair_input,
    spins,
    cotangent,
    w_self,
    w_means,
    w_rows,
    w_cols,
    b_one,
    w_pair,
    b_pair,
):
    highest = lax.Precision.HIGHEST
    walkers, rows_dev, one_width = one_input.shape
    width = pair_input.shape[2]
    electrons = pair_input.shape[3]
    layers = w_self.shape[0]
    flat = walkers * rows_dev
    tall_all = rows_dev * width
    each = math.gcd(rows_dev, 8)
    tall = each * width
    row_start = lax.axis_index("row") * rows_dev

    up_mask = (spins == 1).astype(F32)
    masks = jnp.stack([up_mask, 1.0 - up_mask], axis=1)
    counts = jnp.sum(masks, axis=2)
    own_spins = lax.dynamic_slice_in_dim((spins == 1).astype(jnp.int32), row_start, rows_dev, 1)
    own_mask = lax.dynamic_slice_in_dim(masks, row_start, rows_dev, 2)
    own_up = own_mask[:, 0, :, None] > 0.5

    eye = jnp.eye(each, dtype=BF16)
    mix = jnp.stack([jnp.kron(eye, w_pair[k].T) for k in range(layers - 1)])
    mix_back = jnp.stack([jnp.kron(eye, w_pair[k]) for k in range(layers - 1)])
    bias_tall = jnp.tile(b_pair, (1, each))[:, :, None]
    mask_rows = jnp.pad(masks, ((0, 0), (0, 14), (0, 0))).astype(BF16)
    own_rows = jnp.pad(jnp.repeat(own_mask, width, axis=2), ((0, 0), (0, 6), (0, 0)))
    pair_flat = pair_input.reshape(walkers, tall_all, electrons)

    row_sums, col_part = pair_forward(pair_flat, mask_rows, own_rows, mix, bias_tall, width)
    sum_parts = 2 * layers
    col_part = col_part.reshape(sum_parts, walkers // 4, size, rows_dev, 4 * width)
    col_part = jnp.transpose(col_part, (0, 2, 1, 3, 4)).reshape(sum_parts, size, -1, 4 * width)
    walker_eye = jnp.eye(walkers, dtype=F32)
    gather_mask = (walker_eye[:, None, :, None] * own_mask[:, :, None, :]).reshape(
        2 * walkers, flat
    )
    gather_mask = gather_mask.astype(BF16)
    one_cur = one_input.reshape(flat, one_width)
    first_part = jnp.dot(gather_mask, one_cur, preferred_element_type=F32)
    col_sums, first_sums = reduce_scatter(col_part, first_part, size, 0)
    col_sums = col_sums.reshape(layers, walkers // 2, rows_dev, 2, 2 * width)
    col_sums = jnp.transpose(col_sums, (0, 1, 3, 2, 4)).reshape(
        layers, walkers, rows_dev, 2, width
    )
    row_sums = jnp.transpose(
        row_sums[:, :, :2].reshape(walkers, layers, 2, rows_dev, width), (1, 0, 3, 2, 4)
    )
    scale = counts[None, :, None, :, None]
    row_means = (row_sums / scale).astype(BF16).reshape(layers, flat, 2 * width)
    col_means = (col_sums / scale).astype(BF16).reshape(layers, flat, 2 * width)

    w_all = jnp.concatenate([w_self, w_rows, w_cols], axis=1)
    counts_flat = counts.reshape(2 * walkers, 1)

    stored = []
    for layer in range(layers):
        if layer == 0:
            one_sums = first_sums
        else:
            part_one = jnp.dot(gather_mask, one_cur, preferred_element_type=F32)
            one_sums = reduce_small(part_one, size, 1 + layer)
        one_means = (one_sums / counts_flat).astype(BF16).reshape(walkers, 2 * one_width)
        feats = jnp.concatenate([one_cur, row_means[layer], col_means[layer]], axis=1)
        shared = jnp.dot(one_means, w_means[layer], preferred_element_type=F32) + b_one[layer]
        preact = jnp.dot(feats, w_all[layer], preferred_element_type=F32)
        preact = preact.reshape(walkers, rows_dev, one_width) + shared[:, None, :]
        activation = jnp.tanh(preact)
        stored.append((feats, one_means, activation))
        one_cur = (activation + one_cur.reshape(preact.shape).astype(F32)).astype(BF16)
        one_cur = one_cur.reshape(flat, one_width)
    one_output = one_cur.reshape(walkers, rows_dev, one_width)

    grad_one = cotangent
    feat_grads = [None] * layers
    pre_totals = [None] * layers
    row_parts = []
    col_parts = []
    for layer in reversed(range(layers)):
        feats, one_means, activation = stored[layer]
        grad_pre = (grad_one * (1.0 - activation * activation)).astype(BF16)
        pre_sums = jnp.sum(grad_pre.astype(F32), axis=1)
        flat_pre = grad_pre.reshape(flat, one_width)
        feat_grads[layer] = lax.dot_general(
            feats, flat_pre, (((0,), (0,)), ((), ())), preferred_element_type=F32
        )
        if layer == 0:
            pre_totals[0] = pre_sums
            break
        grad_feat = lax.dot_general(
            flat_pre, w_all[layer], (((1,), (1,)), ((), ())), preferred_element_type=F32
        ).reshape(walkers, rows_dev, one_width + 4 * width)
        side_scale = counts[:, None, :, None]
        row_grad = grad_feat[:, :, one_width : one_width + 2 * width]
        row_grad = row_grad.reshape(walkers, rows_dev, 2, width) / side_scale
        row_parts.append(jnp.transpose(row_grad, (0, 2, 1, 3)).reshape(walkers, 2, tall_all))
        col_grad = grad_feat[:, :, one_width + 2 * width :]
        col_grad = (col_grad.reshape(walkers, rows_dev, 2, width) / side_scale).reshape(
            walkers // 2, 2, rows_dev, 2 * width
        )
        col_parts.append(jnp.transpose(col_grad, (0, 2, 1, 3)).reshape(-1, 4 * width))
        if layer == 1:
            col_all, pre_totals[layer] = all_gather(
                jnp.concatenate([col_parts[1], col_parts[0]]).reshape(4, -1, 4 * width),
                pre_sums,
                size,
                2 + 2 * layers,
            )
        else:
            pre_totals[layer] = reduce_small(pre_sums, size, 1 + layers + layer)
        mean_total = jnp.einsum(
            "wh,ah->wa", pre_totals[layer], w_means[layer].astype(F32), precision=highest
        )
        mean_total = mean_total.reshape(walkers, 2, one_width) / counts[:, :, None]
        grad_one = (
            grad_one
            + grad_feat[:, :, :one_width]
            + jnp.where(own_up, mean_total[:, None, 0], mean_total[:, None, 1])
        )

    row_stack = jnp.concatenate(
        [row_parts[1], row_parts[0], jnp.zeros((walkers, 4, tall_all), F32)], axis=1
    )
    col_all = col_all.reshape(4, size, walkers // 4, rows_dev, 4 * width)
    col_all = jnp.transpose(col_all, (0, 2, 1, 3, 4)).reshape(
        2, walkers // 2, electrons, 4 * width
    )
    lower = jnp.pad(masks, ((0, 0), (0, 6), (0, 0)))
    upper = jnp.pad(masks, ((0, 0), (2, 4), (0, 0)))
    mask_pairs = jnp.stack(
        [
            jnp.concatenate([piece, piece, piece, jnp.zeros_like(piece)], axis=1)
            for piece in (lower, upper)
        ],
        axis=1,
    ).astype(BF16)
    gw, gb, feat_sums = pair_backward(
        own_spins,
        pair_flat,
        mask_pairs,
        row_stack,
        col_all,
        mix,
        mix_back,
        bias_tall,
        jnp.concatenate(feat_grads, axis=0),
        width,
        size,
        3 + 2 * layers,
    )
    g_wpair = jnp.einsum("lacad->lcd", gw.reshape(layers - 1, each, width, each, width))
    g_bpair = jnp.sum(gb, axis=2)

    tail = jnp.concatenate([g_wpair.reshape(-1), g_bpair.reshape(-1)])
    unit = 8 * one_width
    tail = jnp.pad(tail, (0, -tail.size % unit)).reshape(-1, one_width)
    ends = reduce_small(jnp.concatenate([pre_totals[0], tail], axis=0), size, 4 + 2 * layers)
    deep = one_width + 4 * width
    first = feat_sums[: layers * deep].reshape(layers, deep, one_width)
    pre_totals[0] = ends[:walkers]
    tail = ends[walkers:].reshape(-1)
    square = width * width
    pre_all = jnp.stack(pre_totals)
    means_all = jnp.stack([item[1] for item in stored]).astype(F32)
    grad_means = jnp.einsum("lwa,lwk->lak", means_all, pre_all, precision=highest)
    count = layers - 1
    return (
        one_output,
        first[:, :one_width],
        grad_means,
        first[:, one_width : one_width + 2 * width],
        first[:, one_width + 2 * width :],
        jnp.sum(pre_all, axis=1),
        tail[: count * square].reshape(count, width, width),
        tail[count * square : count * square + count * width].reshape(count, width),
    )


def iota(shape, dim):
    return lax.broadcasted_iota(jnp.int32, shape, dim)


def split3(x):
    high = x.astype(BF16).astype(F32)
    rest = x - high
    mid = rest.astype(BF16).astype(F32)
    return jnp.concatenate([high, mid, rest - mid], axis=0).astype(BF16)


class Place:
    def __init__(self, far):
        self.far = far
        self.me, self.core, self.side, self.high = position()
        self.low = lax.rem(self.me, 4)
        self.peer_core = self.me + 1 - 2 * self.core
        self.peer_side = self.me + 2 - 4 * self.side
        self.far_ids = [
            (d, lax.rem(self.high + d + 1, far), lax.rem(self.high + d + 1, far) * 4 + self.low)
            for d in range(far - 1)
        ]
        self.near_ids = [(d, self.high * 4 + lax.rem(self.low + d + 1, 4)) for d in range(3)]


def remote(src, dst, send_sem, recv_sem, target):
    return pltpu.make_async_remote_copy(
        src_ref=src,
        dst_ref=dst,
        send_sem=send_sem,
        recv_sem=recv_sem,
        device_id={"row": target},
        device_id_type=MESH,
    )


class SmallSum:
    def __init__(self, place, across, within, sems):
        self.place, self.across, self.within = place, across, within
        self.sems = sems

    def far_copies(self, k):
        sf, rf, _, _ = self.sems
        mine = self.across.at[k, self.place.high]
        return [
            remote(mine, mine, sf.at[k, d], rf.at[k, d], target)
            for d, _, target in self.place.far_ids
        ]

    def near_copies(self, k):
        _, _, sn, rn = self.sems
        mine = self.within.at[k, self.place.low]
        return [
            remote(mine, mine, sn.at[k, d], rn.at[k, d], target)
            for d, target in self.place.near_ids
        ]

    def start(self, k, value):
        self.across[k, self.place.high] = value
        for copy in self.far_copies(k):
            copy.start()

    def middle(self, k):
        for copy in self.far_copies(k):
            copy.wait()
        total = self.across[k, 0]
        for n in range(1, self.place.far):
            total = total + self.across[k, n]
        self.within[k, self.place.low] = total
        for copy in self.near_copies(k):
            copy.start()

    def finish(self, k):
        for copy in self.near_copies(k):
            copy.wait()
        total = self.within[k, 0]
        for n in range(1, 4):
            total = total + self.within[k, n]
        return total


class ColumnSums:
    def __init__(self, place, source, half, quarter, landed, total, sems):
        self.place, self.source, self.half, self.quarter = place, source, half, quarter
        self.landed, self.total, self.sems = landed, total, sems

    def first(self, k):
        sa, ra = self.sems[0:2]
        p = self.place
        return remote(
            self.source.at[k, :, :, 1 - p.core], self.half.at[k], sa.at[k], ra.at[k], p.peer_core
        )

    def second(self, k):
        sb, rb = self.sems[2:4]
        p = self.place
        return remote(
            self.half.at[k, :, 1 - p.side], self.quarter.at[k], sb.at[k], rb.at[k], p.peer_side
        )

    def third(self, k):
        sc, rc = self.sems[4:6]
        return [
            remote(
                self.quarter.at[k, z], self.landed.at[k, d], sc.at[k, d], rc.at[k, d], target
            )
            for d, z, target in self.place.far_ids
        ]

    def a(self, k):
        self.first(k).start()

    def b(self, k):
        self.first(k).wait()
        self.half[k] = self.half[k] + self.source[k, :, :, self.place.core]
        self.second(k).start()

    def c(self, k):
        self.second(k).wait()
        self.quarter[k] = self.quarter[k] + self.half[k, :, self.place.side]
        for copy in self.third(k):
            copy.start()

    def d(self, k):
        for copy in self.third(k):
            copy.wait()
        total = self.quarter[k, self.place.high]
        for n in range(self.place.far - 1):
            total = total + self.landed[k, n]
        self.total[k] = total


class Gather:
    def __init__(self, place, ref, sems):
        self.place, self.ref, self.sems = place, ref, sems

    def copies(self, k, phase):
        p = self.place
        sa, ra, sb, rb, sc, rc = self.sems
        if phase == 0:
            mine = self.ref.at[k, p.high, p.side, p.core]
            return [
                remote(mine, mine, sa.at[k, d], ra.at[k, d], target)
                for d, _, target in p.far_ids
            ]
        if phase == 1:
            block = self.ref.at[k, :, p.side, p.core]
            return [remote(block, block, sb.at[k], rb.at[k], p.peer_side)]
        block = self.ref.at[k, :, :, p.core]
        return [remote(block, block, sc.at[k], rc.at[k], p.peer_core)]

    def step(self, k, phase):
        if phase > 0:
            for copy in self.copies(k, phase - 1):
                copy.wait()
        if phase < 3:
            for copy in self.copies(k, phase):
                copy.start()


def whole_kernel(
    dims,
    one_ref,
    pair_hbm,
    spins_ref,
    cot_ref,
    wself_ref,
    wmeans_ref,
    wrows_ref,
    wcols_ref,
    bone_ref,
    wpair_ref,
    bpair_ref,
    oneout_ref,
    gself_ref,
    gmeans_ref,
    grows_ref,
    gcols_ref,
    gbias_ref,
    gtail_ref,
    pair0,
    pair1,
    slope0,
    slope1,
    pair2,
    mask16,
    sel,
    mix,
    mix_back,
    bias,
    wbig,
    gmask,
    upcol,
    coef,
    cg,
    cnt_y,
    ysum,
    means,
    feats,
    act,
    grad_one,
    col_two,
    rhs,
    gw,
    cs_source,
    cs_half,
    cs_quarter,
    cs_landed,
    cs_total,
    ag_ref,
    fs_across,
    fs_within,
    bs_across,
    bs_within,
    es_across,
    es_within,
    feat_ref,
    feat_half,
    feat_quarter,
    feat_landed,
    feat_all,
    load_sem,
    *sems,
):
    walkers, rows, width, electrons, one_width, layers, far, tall = dims
    flat = walkers * rows
    tall_all = rows * width
    chunks = tall_all // tall
    each = tall // width
    pairs = walkers // 2
    place = Place(far)

    loads = [
        pltpu.make_async_copy(pair_hbm.at[w], pair0.at[w], load_sem.at[w]) for w in range(walkers)
    ]
    for load in loads:
        load.start()

    barrier = pltpu.get_barrier_semaphore()
    peers = [t for _, _, t in place.far_ids] + [t for _, t in place.near_ids]
    for target in peers:
        pl.semaphore_signal(barrier, inc=1, device_id={"row": target}, device_id_type=MESH)

    sems = list(sems)

    def take(n):
        got = sems[:n]
        del sems[:n]
        return got

    columns = ColumnSums(place, cs_source, cs_half, cs_quarter, cs_landed, cs_total, take(6))
    gather = Gather(place, ag_ref, take(6))
    fwd_sum = SmallSum(place, fs_across, fs_within, take(4))
    bwd_sum = SmallSum(place, bs_across, bs_within, take(4))
    end_sum = SmallSum(place, es_across, es_within, take(4))
    feat_sems = take(12)

    up = (spins_ref[...] == 1).astype(F32)
    down = 1.0 - up
    count_up = jnp.sum(up, axis=1, keepdims=True)
    count_down = jnp.sum(down, axis=1, keepdims=True)
    counts16 = jnp.concatenate([count_up, count_down], axis=0)
    both_spins = jnp.concatenate([up, down], axis=0).astype(BF16)
    first_row = place.me * rows

    pick = (iota((electrons, flat), 0) == first_row + lax.rem(iota((electrons, flat), 1), rows))
    own = contract(both_spins, pick.astype(BF16), 1, 0)
    same = lax.rem(iota((2 * walkers, flat), 0), walkers) == iota((2 * walkers, flat), 1) // rows
    gmask[...] = jnp.where(same, own, 0.0).astype(BF16)
    fwd_partial = contract(gmask[...], one_ref[...], 1, 0)
    pl.semaphore_wait(barrier, len(peers))
    fwd_sum.start(0, fwd_partial)

    lane = iota((width, tall), 1)
    eye_tall = (lax.rem(iota((tall, width), 0), width) == iota((tall, width), 1)).astype(BF16)
    same_block = iota((tall, tall), 0) // width == iota((tall, tall), 1) // width
    for k in range(layers - 1):
        for target, dim in ((mix, 1), (mix_back, 0)):
            part = contract(eye_tall, wpair_ref[k], 1, dim).astype(BF16)
            full = contract(part, eye_tall, 1, 1)
            target[k] = jnp.where(same_block, full, 0.0).astype(BF16)
        bias[k] = jnp.sum(eye_tall.astype(F32) * bpair_ref[k : k + 1, :], axis=1, keepdims=True)

    spread = iota((electrons, tall_all), 0) == first_row + iota((electrons, tall_all), 1) // width
    own_rows = contract(both_spins, spread.astype(BF16), 1, 0)
    eye_wide = (lax.rem(iota((width, tall_all), 1), width) == iota((width, tall_all), 0)).astype(F32)
    row_id = iota((16, electrons), 0)
    for w in range(walkers):
        mask16[w] = jnp.where(
            row_id == 0, up[w : w + 1], jnp.where(row_id == 1, down[w : w + 1], 0.0)
        ).astype(BF16)
        sel[w] = jnp.concatenate(
            [eye_wide * own_rows[w : w + 1], eye_wide * own_rows[walkers + w : walkers + w + 1]],
            axis=0,
        ).astype(BF16)

    def walker_counts(w, lanes, period):
        is_up = lax.rem(iota((1, lanes), 1), 2 * period) < period
        return jnp.where(is_up, count_up[w : w + 1], count_down[w : w + 1])

    for w in range(walkers):
        cg[w] = jnp.broadcast_to(walker_counts(w, 4 * width, width), (rows, 4 * width))
        cnt_y[w] = jnp.broadcast_to(walker_counts(w, 8 * width, 4 * width), (8, 8 * width))
    which = lax.rem(iota((2 * walkers, 4 * width), 1), 2 * width) // width
    chooser = (iota((2 * walkers, 4 * width), 0) // walkers == which).astype(BF16)
    own_cols = contract(gmask[...], chooser, 0, 0)
    for level in range(2):
        coef[level, :, 4 * width :] = own_cols
    is_up_row = (iota((2 * walkers, one_width), 0) < walkers).astype(BF16)
    upcol[...] = contract(gmask[...], is_up_row, 0, 0)
    for k in range(layers):
        wbig[k, :one_width] = wself_ref[k]
        for start, ref in ((0, wrows_ref), (4, wcols_ref)):
            for copy in range(2):
                low = one_width + (start + 2 * copy) * width
                wbig[k, low : low + 2 * width] = ref[k]

    def row_sums(layer, w, chunk, pair):
        got = contract(mask16[w], pair, 1, 1)
        for k in range(tall // 128):
            for s in range(2):
                ysum[layer, w, pl.ds(chunk * (tall // 128) + k, 1), s * 128 : (s + 1) * 128] = got[
                    s : s + 1, k * 128 : (k + 1) * 128
                ]

    def stream(layer, w, slot, source, source_w, slopes, target, target_w):
        cols = None
        for chunk in range(chunks):
            here = slice(chunk * tall, (chunk + 1) * tall)
            pair = source[source_w, here]
            row_sums(layer, w, chunk, pair)
            left = jnp.concatenate([mix[layer], sel[w, :, here]], axis=0)
            both = contract(left, pair, 1, 0)
            part = both[tall:]
            cols = part if cols is None else cols + part
            bend = jnp.tanh(both[:tall] + bias[layer])
            slopes[w, here] = (1.0 - bend * bend).astype(BF16)
            target[target_w, here] = (bend + pair.astype(F32)).astype(BF16)
        col_two[slot] = cols

    def sums_only(layer, w, slot):
        cols = None
        for chunk in range(chunks):
            here = slice(chunk * tall, (chunk + 1) * tall)
            pair = pair2[slot, here]
            row_sums(layer, w, chunk, pair)
            part = contract(sel[w, :, here], pair, 1, 0)
            cols = part if cols is None else cols + part
        col_two[slot] = cols

    def tick(t):
        both = col_two[...].reshape(4 * width, electrons)
        cs_source[t] = both.T.reshape(far, 2, 2, rows, 4 * width)
        columns.a(t)
        for lag, step in ((1, columns.b), (2, columns.c), (3, columns.d)):

            @pl.when(t >= lag)
            def _(lag=lag, step=step):
                step(t - lag)

    def part_of(layer, p):
        return p if layer == 0 else pairs + 2 * p + layer - 1

    def one_layer(layer):
        totals = fwd_sum.finish(layer)
        mean = (totals / counts16).astype(BF16)
        means[layer] = mean
        ups = contract(mean, wmeans_ref[layer, :one_width], 1, 0)
        downs = contract(mean, wmeans_ref[layer, one_width:], 1, 0)
        shared = ups[:walkers] + downs[walkers:] + bone_ref[layer : layer + 1, :]
        lanes = 8 * width
        ys = (ysum[layer] / cnt_y[...]).reshape(walkers * 8, lanes).astype(BF16)
        per = rows // 8
        expand = iota((flat, walkers * 8), 0) // per == iota((flat, walkers * 8), 1)
        wide = contract(expand.astype(BF16), ys, 1, 0)
        keep = lax.rem(iota((flat, lanes), 1) // width, 4) == lax.rem(iota((flat, lanes), 0), per)
        wide = jnp.where(keep, wide, 0.0).astype(BF16)
        src, dst = iota((lanes, 4 * width), 0), iota((lanes, 4 * width), 1)
        fold = (src // (4 * width)) * width + lax.rem(src, width) == dst
        row_mean = contract(wide, fold.astype(BF16), 1, 0)
        first_half = iota((rows, 4 * width), 1) < 2 * width
        col_mean = []
        for p in range(pairs):
            total = cs_total[part_of(layer, p)]
            col_mean.append(jnp.where(first_half, total / cg[2 * p], 0.0))
            col_mean.append(jnp.where(first_half, 0.0, total / cg[2 * p + 1]))
        current = one_ref[...] if layer == 0 else oneout_ref[...]
        feats[layer, :, :one_width] = current
        feats[layer, :, one_width : one_width + 4 * width] = row_mean.astype(BF16)
        feats[layer, :, one_width + 4 * width :] = jnp.concatenate(col_mean, axis=0).astype(BF16)
        preact = contract(feats[layer], wbig[layer], 1, 0)
        for w in range(walkers):
            here = slice(w * rows, (w + 1) * rows)
            bend = jnp.tanh(preact[here] + shared[w : w + 1])
            act[layer, here] = bend
            oneout_ref[here] = (bend + current[here].astype(F32)).astype(BF16)
        if layer + 1 < layers:
            fwd_sum.start(layer + 1, contract(gmask[...], oneout_ref[...], 1, 0))

    def load_wait(w):
        for k in range(walkers):

            @pl.when(w == k)
            def _(k=k):
                loads[k].wait()

    def pass0(p, carry):
        def body(slot, inner):
            w = 2 * p + slot
            load_wait(w)
            stream(0, w, slot, pair0, w, slope0, pair1, w)
            return inner

        lax.fori_loop(0, 2, body, 0)
        tick(p)

        @pl.when(p == 1)
        def _():
            fwd_sum.middle(0)

        return carry

    lax.fori_loop(0, pairs, pass0, 0)

    def pass1(p, carry):
        def body(slot, inner):
            w = 2 * p + slot
            stream(1, w, slot, pair1, w, slope1, pair2, slot)
            return inner

        lax.fori_loop(0, 2, body, 0)
        tick(pairs + 2 * p)

        def body2(slot, inner):
            sums_only(2, 2 * p + slot, slot)
            return inner

        lax.fori_loop(0, 2, body2, 0)
        tick(pairs + 2 * p + 1)

        @pl.when(p == 1)
        def _():
            one_layer(0)

        @pl.when(p == 2)
        def _():
            fwd_sum.middle(1)

        return carry

    lax.fori_loop(0, pairs, pass1, 0)
    parts = pairs * layers
    columns.b(parts - 1)
    columns.c(parts - 2)
    columns.d(parts - 3)
    columns.c(parts - 1)
    columns.d(parts - 2)
    columns.d(parts - 1)
    one_layer(1)
    fwd_sum.middle(2)
    one_layer(2)

    walker_sum = (iota((16, flat), 0) == iota((16, flat), 1) // rows).astype(BF16)
    blocks = 4 * far
    deep = one_width + 4 * width
    block_rows = deep // blocks

    def cotangents(layer, level):
        grad = cot_ref[...] if layer == layers - 1 else grad_one[...]
        bend = act[layer]
        pre = (grad * (1.0 - bend * bend)).astype(BF16)
        index = layers - 1 - layer
        bwd_sum.start(index, contract(walker_sum, pre, 1, 0)[:walkers])
        if layer > 0:
            back = contract(pre, wbig[layer], 1, 1)
            grad_one[...] = grad + back[:, :one_width]
            counts = cg[...].reshape(flat, 4 * width)
            col = back[:, one_width + 4 * width :] / counts
            first_half = iota((rows, 4 * width), 1) < 2 * width
            for p in range(pairs):
                even = col[2 * p * rows : (2 * p + 1) * rows]
                odd = col[(2 * p + 1) * rows : (2 * p + 2) * rows]
                ag_ref[level, place.high, place.side, place.core, p] = jnp.where(
                    first_half, even, odd
                )
            gather.step(level, 0)
            row = back[:, one_width : one_width + 4 * width] / counts
            if layer < layers - 1:
                row = row + coef[1 - level, :, : 4 * width]
            coef[level, :, : 4 * width] = row
        grads = contract(feats[layer], pre, 0, 0)
        cols_at = one_width + 4 * width
        kept = jnp.concatenate(
            [
                grads[: one_width + 2 * width],
                grads[cols_at : cols_at + 2 * width] + grads[cols_at + 2 * width :],
            ],
            axis=0,
        )
        for b in range(blocks):
            feat_ref[b // 4, (b // 2) % 2, b % 2, layer] = kept[b * block_rows : (b + 1) * block_rows]

    def finish_pre(layer):
        total = bwd_sum.finish(layers - 1 - layer)
        pieces = split3(total)
        mean = means[layer].astype(F32)
        for s in range(2):
            piece = mean[s * walkers : (s + 1) * walkers]
            tripled = jnp.concatenate([piece, piece, piece], axis=0).astype(BF16)
            gmeans_ref[layer, s * one_width : (s + 1) * one_width] = contract(tripled, pieces, 0, 0)
        gbias_ref[layer] = jnp.sum(total, axis=0, keepdims=True)
        return pieces

    def spread_means(layer):
        pieces = finish_pre(layer)
        back = contract(pieces, wmeans_ref[layer], 1, 1)
        total = back[:walkers] + back[walkers : 2 * walkers] + back[2 * walkers :]
        mean_up = total[:, :one_width] / count_up
        mean_down = total[:, one_width:] / count_down
        for w in range(walkers):
            here = slice(w * rows, (w + 1) * rows)
            grad_one[here] = grad_one[here] + jnp.where(
                upcol[here] > 0.5, mean_up[w : w + 1], mean_down[w : w + 1]
            )

    cotangents(2, 0)
    bwd_sum.middle(0)
    gather.step(0, 1)
    spread_means(2)
    cotangents(1, 1)
    bwd_sum.middle(1)
    gather.step(0, 2)
    gather.step(1, 1)
    spread_means(1)
    cotangents(0, 0)

    first_half = iota((flat, 4 * width), 1) < 2 * width
    for level in range(2):
        row = coef[level, :, : 4 * width]
        lead = row.astype(BF16).astype(F32)
        coef[level, :, : 4 * width] = jnp.where(first_half, lead, row - lead)

    bwd_sum.middle(2)
    gw[...] = jnp.zeros_like(gw)
    gather.step(0, 3)

    lane_eye = (
        lax.rem(iota((width, 8 * width), 1), width) == iota((width, 8 * width), 0)
    ).astype(F32)
    ones = jnp.ones((16, electrons), BF16)
    spin_of = lax.rem(iota((4 * width, electrons), 0), 2 * width) < width

    def prepare(level, p):
        turned = []
        for n in range(level + 1):
            block = ag_ref[n, :, :, :, p].reshape(electrons, 4 * width)
            turned.append(block)
        total = turned[0] if level == 0 else turned[0] + turned[1]
        total = total.T
        for slot in range(2):
            mine = total[slot * 2 * width : (slot + 1) * 2 * width]
            lead = mine.astype(BF16)
            rhs[slot, 4 * width : 6 * width] = lead
            rhs[slot, 6 * width :] = (mine - lead.astype(F32)).astype(BF16)
            spins = mask16[2 * p + slot].astype(F32)
            rhs[slot, : 4 * width] = jnp.where(spin_of, spins[0:1], spins[1:2]).astype(BF16)

    def spread_coef(level, w, chunk):
        pieces = []
        for e in range(each):
            line = coef[level, pl.ds(w * rows + chunk * each + e, 1), :]
            pieces.append(lane_eye * line)
        return jnp.concatenate(pieces, axis=0).astype(BF16)

    def level_one(p, slot):
        w = 2 * p + slot
        for chunk in range(chunks):
            here = slice(chunk * tall, (chunk + 1) * tall)
            grad = contract(spread_coef(0, w, chunk), rhs[slot], 1, 0)
            gz = (grad * slope1[w, here].astype(F32)).astype(BF16)
            slope1[w, here] = gz
            gw[1] += contract(jnp.concatenate([pair1[w, here], ones], axis=0), gz, 1, 1)

    def level_zero(p, slot):
        w = 2 * p + slot
        for chunk in range(chunks):
            here = slice(chunk * tall, (chunk + 1) * tall)
            left = jnp.concatenate([mix_back[1], spread_coef(1, w, chunk)], axis=1)
            right = jnp.concatenate([slope1[w, here], rhs[slot]], axis=0)
            grad = contract(left, right, 1, 0)
            gz = (grad * slope0[w, here].astype(F32)).astype(BF16)
            gw[0] += contract(jnp.concatenate([pair0[w, here], ones], axis=0), gz, 1, 1)

    def run(level, work, after):
        def step(p, carry):
            prepare(level, p)

            def body(slot, inner):
                work(p, slot)
                return inner

            lax.fori_loop(0, 2, body, 0)
            for at, todo in after:

                @pl.when(p == at)
                def _(todo=todo):
                    todo()

            return carry

        lax.fori_loop(0, pairs, step, 0)

    def feat(phase):
        return lambda: reduce_phase(
            phase, far, feat_ref, feat_all, feat_half, feat_quarter, feat_landed, feat_sems
        )

    def finish_last():
        finish_pre(0)

    run(0, level_one, [(0, lambda: gather.step(1, 2)), (0, finish_last)] + [(k, feat(k - 1)) for k in (1, 2, 3)])
    gather.step(1, 3)
    run(1, level_zero, [(k, feat(k + 3)) for k in range(3)])

    lanes_total = None
    for k in range(layers - 1):
        grid = gw[k]
        folded = jnp.zeros((width, tall), F32)
        for a in range(each):
            folded = folded + jnp.where(
                lane // width == a, grid[a * width : (a + 1) * width], 0.0
            )
        folded = jnp.concatenate([folded, grid[tall : tall + 8]], axis=0)
        src, dst = iota((tall, 128), 0), iota((tall, 128), 1)
        fold = (lax.rem(src, width) + k * width == dst).astype(BF16)
        pieces = contract(split3(folded), fold, 1, 0)
        size = width + 8
        piece = pieces[:size] + pieces[size : 2 * size] + pieces[2 * size :]
        lanes_total = piece if lanes_total is None else lanes_total + piece
    end_sum.start(0, lanes_total)
    feat(6)()
    end_sum.middle(0)
    for layer in range(layers):
        for b in range(blocks):
            block = feat_all[b // 4, (b // 2) % 2, b % 2, layer]
            for piece in range(block_rows // 8):
                at = b * block_rows + piece * 8
                value = block[piece * 8 : (piece + 1) * 8]
                if at < one_width:
                    gself_ref[layer, at : at + 8] = value
                elif at < one_width + 2 * width:
                    at = at - one_width
                    grows_ref[layer, at : at + 8] = value
                else:
                    at = at - one_width - 2 * width
                    gcols_ref[layer, at : at + 8] = value
    gtail_ref[...] = end_sum.finish(0)


def local(
    size,
    one_input,
    pair_input,
    spins,
    cotangent,
    w_self,
    w_means,
    w_rows,
    w_cols,
    b_one,
    w_pair,
    b_pair,
):
    walkers, rows, one_width = one_input.shape
    width, electrons = pair_input.shape[2:]
    layers = w_self.shape[0]
    far = size // 4
    if rows * width != 1024 or width != 32 or walkers != 8 or layers != 3 or far < 2:
        return general(
            size,
            one_input,
            pair_input,
            spins,
            cotangent,
            w_self,
            w_means,
            w_rows,
            w_cols,
            b_one,
            w_pair,
            b_pair,
        )
    flat = walkers * rows
    tall_all = rows * width
    tall = 8 * width
    pairs = walkers // 2
    parts = layers * pairs
    deep = one_width + 4 * width
    block = deep // size
    lanes = 4 * width
    dims = (walkers, rows, width, electrons, one_width, layers, far, tall)
    vmem = pltpu.VMEM
    scratch = [
        vmem((walkers, tall_all, electrons), BF16),
        vmem((walkers, tall_all, electrons), BF16),
        vmem((walkers, tall_all, electrons), BF16),
        vmem((walkers, tall_all, electrons), BF16),
        vmem((2, tall_all, electrons), BF16),
        vmem((walkers, 16, electrons), BF16),
        vmem((walkers, 2 * width, tall_all), BF16),
        vmem((layers - 1, tall, tall), BF16),
        vmem((layers - 1, tall, tall), BF16),
        vmem((layers - 1, tall, 1), F32),
        vmem((layers, one_width + 2 * lanes, one_width), BF16),
        vmem((2 * walkers, flat), BF16),
        vmem((flat, one_width), F32),
        vmem((2, flat, 2 * lanes), F32),
        vmem((walkers, rows, lanes), F32),
        vmem((walkers, 8, 2 * lanes), F32),
        vmem((layers, walkers, 8, 2 * lanes), F32),
        vmem((layers, 2 * walkers, one_width), BF16),
        vmem((layers, flat, one_width + 2 * lanes), BF16),
        vmem((layers, flat, one_width), F32),
        vmem((flat, one_width), F32),
        vmem((2, 2 * width, electrons), F32),
        vmem((2, 2 * lanes, electrons), BF16),
        vmem((2, tall + 16, tall), F32),
        vmem((parts, far, 2, 2, rows, lanes), F32),
        vmem((parts, far, 2, rows, lanes), F32),
        vmem((parts, far, rows, lanes), F32),
        vmem((parts, far - 1, rows, lanes), F32),
        vmem((parts, rows, lanes), F32),
        vmem((2, far, 2, 2, pairs, rows, lanes), F32),
        vmem((layers, far, 2 * walkers, one_width), F32),
        vmem((layers, 4, 2 * walkers, one_width), F32),
        vmem((layers, far, walkers, one_width), F32),
        vmem((layers, 4, walkers, one_width), F32),
        vmem((1, far, width + 8, 128), F32),
        vmem((1, 4, width + 8, 128), F32),
        vmem((far, 2, 2, layers, block, one_width), F32),
        vmem((far, 2, layers, block, one_width), F32),
        vmem((far, layers, block, one_width), F32),
        vmem((far, layers, block, one_width), F32),
        vmem((far, 2, 2, layers, block, one_width), F32),
    ]
    scratch += dma((walkers,))
    scratch += dma((parts,), (parts,), (parts,), (parts,), (parts, far), (parts, far))
    scratch += dma((2, far), (2, far), (2,), (2,), (2,), (2,))
    scratch += dma(*([(layers, far), (layers, far), (layers, 4), (layers, 4)] * 2))
    scratch += dma((1, far), (1, far), (1, 4), (1, 4))
    scratch += dma((1,), (1,), (1,), (1,), (far,), (far,), (far,), (far,), (1,), (1,), (1,), (1,))
    in_vmem = pl.BlockSpec(memory_space=pltpu.VMEM)
    shape = jax.ShapeDtypeStruct
    out = pl.pallas_call(
        functools.partial(whole_kernel, dims),
        out_shape=(
            shape((flat, one_width), BF16),
            shape((layers, one_width, one_width), F32),
            shape((layers, 2 * one_width, one_width), F32),
            shape((layers, 2 * width, one_width), F32),
            shape((layers, 2 * width, one_width), F32),
            shape((layers, 1, one_width), F32),
            shape((width + 8, 128), F32),
        ),
        in_specs=[in_vmem, pl.BlockSpec(memory_space=pl.ANY)] + [in_vmem] * 9,
        out_specs=(in_vmem,) * 7,
        scratch_shapes=scratch,
        compiler_params=pltpu.CompilerParams(
            vmem_limit_bytes=60 * 1024 * 1024, collective_id=0, has_side_effects=True
        ),
    )(
        one_input.reshape(flat, one_width),
        pair_input.reshape(walkers, tall_all, electrons),
        spins,
        cotangent.reshape(flat, one_width),
        w_self,
        w_means,
        w_rows,
        w_cols,
        b_one,
        w_pair,
        b_pair,
    )
    one_out, g_self, g_means, g_rows, g_cols, g_bias, tail = out
    return (
        one_out.reshape(walkers, rows, one_width),
        g_self,
        g_means,
        g_rows,
        g_cols,
        g_bias.reshape(layers, one_width),
        jnp.stack([tail[:width, k * width : (k + 1) * width] for k in range(layers - 1)]),
        jnp.stack([tail[width, k * width : (k + 1) * width] for k in range(layers - 1)]),
    )


def solution(mesh):
    in_specs = (
        P("group", "row", None),
        P("group", "row", None, None),
        P("group", None),
        P("group", "row", None),
        P(),
        P(),
        P(),
        P(),
        P(),
        P(),
        P(),
    )
    out_specs = (
        P("group", "row", None),
        P("group", None, None),
        P("group", None, None),
        P("group", None, None),
        P("group", None, None),
        P("group", None),
        P("group", None, None),
        P("group", None),
    )
    return jax.shard_map(
        functools.partial(local, mesh.shape["row"]),
        mesh=mesh,
        in_specs=in_specs,
        out_specs=out_specs,
        check_vma=False,
    )
```

```python
import functools
import math

import jax
import jax.numpy as jnp
from jax import lax
from jax.experimental import pallas as pl
from jax.experimental.pallas import tpu as pltpu
from jax.sharding import PartitionSpec as P

F32 = jnp.float32
BF16 = jnp.bfloat16
MESH = pl.DeviceIdType.MESH
VMEM_LIMIT = 48 * 1024 * 1024


def greet(targets):
    barrier = pltpu.get_barrier_semaphore()
    for target in targets:
        pl.semaphore_signal(barrier, inc=1, device_id={"row": target}, device_id_type=MESH)
    pl.semaphore_wait(barrier, len(targets))


def send(src, dst, send_sem, recv_sem, target):
    copy = pltpu.make_async_remote_copy(
        src_ref=src,
        dst_ref=dst,
        send_sem=send_sem,
        recv_sem=recv_sem,
        device_id={"row": target},
        device_id_type=MESH,
    )
    copy.start()
    return copy


def neighbours(near, far):
    me = lax.axis_index("row")
    low = lax.rem(me, near)
    high = me // near
    near_ids = [high * near + lax.rem(low + k, near) for k in range(1, near)]
    far_ids = [lax.rem(high + k, far) * near + low for k in range(1, far)]
    return low, high, near_ids, far_ids


def small_steps(near, far, x_ref, o_ref, slots, part, slots_far, sn, rn, sf, rf):
    low, high, near_ids, far_ids = neighbours(near, far)
    copies = [
        send(x_ref, slots.at[low], sn.at[k], rn.at[k], target) for k, target in enumerate(near_ids)
    ]
    slots[low] = x_ref[...]
    yield
    for copy in copies:
        copy.wait()
    total = slots[0]
    for k in range(1, near):
        total = total + slots[k]
    part[...] = total
    copies = [
        send(part, slots_far.at[high], sf.at[k], rf.at[k], target)
        for k, target in enumerate(far_ids)
    ]
    slots_far[high] = total
    yield
    for copy in copies:
        copy.wait()
    total = slots_far[0]
    for k in range(1, far):
        total = total + slots_far[k]
    o_ref[...] = total
    yield


def greet_all(near, far):
    low, high, near_ids, far_ids = neighbours(near, far)
    greet(near_ids + far_ids)


def reduce_small_kernel(near, far, *refs):
    greet_all(near, far)
    for _ in small_steps(near, far, *refs):
        pass


def small_scratch(near, far, shape):
    return [
        pltpu.VMEM((near,) + shape, F32),
        pltpu.VMEM(shape, F32),
        pltpu.VMEM((far,) + shape, F32),
        pltpu.SemaphoreType.DMA((near,)),
        pltpu.SemaphoreType.DMA((near,)),
        pltpu.SemaphoreType.DMA((far,)),
        pltpu.SemaphoreType.DMA((far,)),
    ]


def reduce_small(x, size, collective_id):
    near = math.gcd(size, 4)
    far = size // near
    return pl.pallas_call(
        functools.partial(reduce_small_kernel, near, far),
        out_shape=jax.ShapeDtypeStruct(x.shape, F32),
        in_specs=[pl.BlockSpec(memory_space=pltpu.VMEM)],
        out_specs=pl.BlockSpec(memory_space=pltpu.VMEM),
        scratch_shapes=small_scratch(near, far, x.shape),
        compiler_params=pltpu.CompilerParams(collective_id=collective_id, has_side_effects=True),
    )(x)


def position():
    me = lax.axis_index("row")
    return me, lax.rem(me, 2), lax.rem(me // 2, 2), me // 4


def scatter_steps(parts, far, x_ref, half, quarter, landed, sems, small):
    me, core, side, high = position()
    peer_core = me + 1 - 2 * core
    peer_side = me + 2 - 4 * side
    far_ids = [lax.rem(high + k, far) for k in range(1, far)]
    sa, ra, sb, rb, sc, rc = sems
    first, second, third = [], [], []
    for k in range(parts):
        first.append(send(x_ref.at[k, :, :, 1 - core], half.at[k], sa.at[k], ra.at[k], peer_core))
    next(small)
    for k in range(parts):
        first[k].wait()
        half[k] = half[k] + x_ref[k, :, :, core]
        second.append(send(half.at[k, :, 1 - side], quarter.at[k], sb.at[k], rb.at[k], peer_side))
    next(small)
    for k in range(parts):
        second[k].wait()
        quarter[k] = quarter[k] + half[k, :, side]
        third.append(
            [
                send(
                    quarter.at[k, to],
                    landed.at[k, d],
                    sc.at[k, d],
                    rc.at[k, d],
                    to * 4 + lax.rem(me, 4),
                )
                for d, to in enumerate(far_ids)
            ]
        )
    next(small)
    for k in range(parts):
        total = quarter[k, high]
        for d, copy in enumerate(third[k]):
            copy.wait()
            total = total + landed[k, d]
        yield k, total


def gather_steps(parts, far, o_ref, values, sems, small):
    me, core, side, high = position()
    peer_core = me + 1 - 2 * core
    peer_side = me + 2 - 4 * side
    far_ids = [lax.rem(high + k, far) for k in range(1, far)]
    sa, ra, sb, rb, sc, rc = sems
    first, second, third = [], [], []
    for k, value in values:
        o_ref[k, high, side, core] = value
        mine = o_ref.at[k, high, side, core]
        first.append(
            [
                send(mine, mine, sa.at[k, d], ra.at[k, d], to * 4 + lax.rem(me, 4))
                for d, to in enumerate(far_ids)
            ]
        )
    next(small)
    for k in range(parts):
        for copy in first[k]:
            copy.wait()
        block = o_ref.at[k, :, side, core]
        second.append(send(block, block, sb.at[k], rb.at[k], peer_side))
    next(small)
    for k in range(parts):
        second[k].wait()
        block = o_ref.at[k, :, :, core]
        third.append(send(block, block, sc.at[k], rc.at[k], peer_core))
    next(small)
    for k in range(parts):
        third[k].wait()


def scatter_kernel(parts, far, x_ref, y_ref, o_ref, oy_ref, *refs):
    greet_all(4, far)
    small = small_steps(4, far, y_ref, oy_ref, *refs[9:])
    for k, total in scatter_steps(parts, far, x_ref, *refs[:3], refs[3:9], small):
        o_ref[k] = total


def gather_kernel(parts, far, x_ref, y_ref, o_ref, oy_ref, *refs):
    greet_all(4, far)
    small = small_steps(4, far, y_ref, oy_ref, *refs[6:])
    gather_steps(parts, far, o_ref, [(k, x_ref[k]) for k in range(parts)], refs[:6], small)


def reduce_phase(phase, far, x_ref, o_ref, half, quarter, landed, sems):
    me = lax.axis_index("row")
    core, side, high = lax.rem(me, 2), lax.rem(me // 2, 2), me // 4
    peer_core = me + 1 - 2 * core
    peer_side = me + 2 - 4 * side
    far_ids = [(d, lax.rem(high + d + 1, far)) for d in range(far - 1)]

    def copies(which):
        def make(src, dst, slot, target):
            return pltpu.make_async_remote_copy(
                src_ref=src,
                dst_ref=dst,
                send_sem=sems[2 * which].at[slot],
                recv_sem=sems[2 * which + 1].at[slot],
                device_id={"row": target},
                device_id_type=MESH,
            )

        if which == 0:
            return [make(x_ref.at[:, :, 1 - core], half, 0, peer_core)]
        if which == 1:
            return [make(half.at[:, 1 - side], quarter, 0, peer_side)]
        if which == 2:
            return [
                make(quarter.at[to], landed.at[d], d, to * 4 + lax.rem(me, 4)) for d, to in far_ids
            ]
        if which == 3:
            mine = o_ref.at[high, side, core]
            return [make(mine, mine, d, to * 4 + lax.rem(me, 4)) for d, to in far_ids]
        if which == 4:
            return [make(o_ref.at[:, side, core], o_ref.at[:, side, core], 0, peer_side)]
        return [make(o_ref.at[:, :, core], o_ref.at[:, :, core], 0, peer_core)]

    if phase > 0:
        for copy in copies(phase - 1):
            copy.wait()
    if phase == 1:
        half[...] = half[...] + x_ref[:, :, core]
    elif phase == 2:
        quarter[...] = quarter[...] + half[:, side]
    elif phase == 3:
        total = quarter[high]
        for d, _ in far_ids:
            total = total + landed[d]
        o_ref[high, side, core] = total
    if phase < 6:
        for copy in copies(phase):
            copy.start()


def scatter_scratch(parts, far, rows, lanes):
    return [
        pltpu.VMEM((parts, far, 2, rows, lanes), F32),
        pltpu.VMEM((parts, far, rows, lanes), F32),
        pltpu.VMEM((parts, far, rows, lanes), F32),
    ]


def dma(*shapes):
    return [pltpu.SemaphoreType.DMA(shape) for shape in shapes]


def scatter_sems(parts, far):
    return dma((parts,), (parts,), (parts,), (parts,), (parts, far), (parts, far))


def gather_sems(parts, far):
    return dma((parts, far), (parts, far), (parts,), (parts,), (parts,), (parts,))


def comm_call(kernel, x, y, out_shape, scratch, collective_id):
    return pl.pallas_call(
        kernel,
        out_shape=(jax.ShapeDtypeStruct(out_shape, F32), jax.ShapeDtypeStruct(y.shape, F32)),
        in_specs=[pl.BlockSpec(memory_space=pltpu.VMEM)] * 2,
        out_specs=(pl.BlockSpec(memory_space=pltpu.VMEM),) * 2,
        scratch_shapes=scratch,
        compiler_params=pltpu.CompilerParams(
            collective_id=collective_id, has_side_effects=True, vmem_limit_bytes=VMEM_LIMIT
        ),
    )(x, y)


def reduce_scatter(x, y, size, collective_id):
    parts, _, rows, lanes = x.shape
    far = size // 4
    return comm_call(
        functools.partial(scatter_kernel, parts, far),
        x.reshape(parts, far, 2, 2, rows, lanes),
        y,
        (parts, rows, lanes),
        scatter_scratch(parts, far, rows, lanes)
        + scatter_sems(parts, far)
        + small_scratch(4, far, y.shape),
        collective_id,
    )


def all_gather(x, y, size, collective_id):
    parts, rows, lanes = x.shape
    far = size // 4
    out, total = comm_call(
        functools.partial(gather_kernel, parts, far),
        x,
        y,
        (parts, far, 2, 2, rows, lanes),
        gather_sems(parts, far) + small_scratch(4, far, y.shape),
        collective_id,
    )
    return out.reshape(parts, size, rows, lanes), total


def contract(a, b, dim_a, dim_b):
    return lax.dot_general(a, b, (((dim_a,), (dim_b,)), ((), ())), preferred_element_type=F32)


def forward_kernel(width, chunks, x_ref, mask_ref, own_ref, mix_ref, bias_ref, row_ref, col_ref):
    stream_layers = mix_ref.shape[0]
    tall = mix_ref.shape[1]
    lane = lax.broadcasted_iota(jnp.int32, (width, tall), 1)
    sub = lax.broadcasted_iota(jnp.int32, (width, tall), 0)
    eye = (lax.rem(lane, width) == sub).astype(F32)
    sums = [[], []]
    for walker in range(2):
        spin_rows = mask_ref[walker]
        cols = [None] * (stream_layers + 1)
        for chunk in range(chunks):
            here = slice(chunk * tall, (chunk + 1) * tall)
            own = own_ref[walker, :, here]
            select = jnp.concatenate([eye * own[0:1], eye * own[1:2]], axis=0).astype(BF16)
            pair = x_ref[walker, here]
            for layer in range(stream_layers + 1):
                row_ref[walker, layer, :, here] = contract(spin_rows, pair, 1, 1)[:8]
                part = contract(select, pair, 1, 0)
                cols[layer] = part if chunk == 0 else cols[layer] + part
                if layer < stream_layers:
                    zvals = contract(mix_ref[layer], pair, 1, 0)
                    bend = jnp.tanh(zvals + bias_ref[layer])
                    pair = (bend + pair.astype(F32)).astype(BF16)
        sums[walker] = cols
    for layer in range(stream_layers + 1):
        both = jnp.concatenate([sums[0][layer], sums[1][layer]], axis=0)
        col_ref[layer, 0] = both.T


def pair_forward(pair, mask_rows, own_rows, mix, bias_tall, width):
    walkers, tall_all, electrons = pair.shape
    layers = mix.shape[0] + 1
    chunks = tall_all // mix.shape[1]
    return pl.pallas_call(
        functools.partial(forward_kernel, width, chunks),
        grid=(walkers // 2,),
        out_shape=(
            jax.ShapeDtypeStruct((walkers, layers, 8, tall_all), F32),
            jax.ShapeDtypeStruct((layers, walkers // 2, electrons, 4 * width), F32),
        ),
        in_specs=[
            pl.BlockSpec((2, tall_all, electrons), lambda w: (w, 0, 0)),
            pl.BlockSpec((2,) + mask_rows.shape[1:], lambda w: (w, 0, 0)),
            pl.BlockSpec((2, 8, tall_all), lambda w: (w, 0, 0)),
            pl.BlockSpec(mix.shape, lambda w: (0, 0, 0)),
            pl.BlockSpec(bias_tall.shape, lambda w: (0, 0, 0)),
        ],
        out_specs=(
            pl.BlockSpec((2, layers, 8, tall_all), lambda w: (w, 0, 0, 0)),
            pl.BlockSpec((layers, 1, electrons, 4 * width), lambda w: (0, w, 0, 0)),
        ),
        compiler_params=pltpu.CompilerParams(vmem_limit_bytes=VMEM_LIMIT),
    )(pair, mask_rows, own_rows, mix, bias_tall)


def backward_kernel(
    width,
    chunks,
    far,
    x_steps,
    spin_ref,
    x_ref,
    mask_ref,
    row_ref,
    col_ref,
    mix_ref,
    mix_back_ref,
    bias_ref,
    feat_ref,
    gw_ref,
    gb_ref,
    sum_ref,
    turned,
    half,
    quarter,
    landed,
    gathered,
    *sems,
):
    walker = pl.program_id(0)
    slots = x_steps * chunks
    starts = [slots * share // 32 for share in (0, 2, 9, 16, 23, 30)]

    tall = mix_ref.shape[1]
    electrons = x_ref.shape[2]
    each = tall // width
    parity = lax.rem(walker, 2)

    @pl.when(walker == 0)
    def _():
        gw_ref[...] = jnp.zeros_like(gw_ref)
        gb_ref[...] = jnp.zeros_like(gb_ref)

    @pl.when(parity == 0)
    def _():
        for level in range(2):
            turned[level] = col_ref[level, 0].T.reshape(4, width, electrons)

    def grad_mean(level, chunk):
        here = slice(chunk * tall, (chunk + 1) * tall)
        row = row_ref[0, :, here]
        high = row.astype(BF16).astype(F32)
        rest = row - high
        mid = rest.astype(BF16).astype(F32)
        low = rest - mid
        split = jnp.concatenate([high, mid, low, jnp.zeros_like(row)], axis=0).astype(BF16)
        rows = contract(split, mask_ref[0, level], 0, 0)
        cols = []
        for step in range(each):
            spin = spin_ref[walker, chunk * each + step]
            cols.append(turned[level, parity * 2 + 1 - spin])
        return rows + jnp.concatenate(cols, axis=0)

    for chunk in range(chunks):
        for phase, start in enumerate(starts):
            if start % chunks == chunk:

                @pl.when(walker == start // chunks)
                def _(phase=phase):
                    if phase == 0:
                        greet_all(4, far)
                    reduce_phase(phase, far, feat_ref, gathered, half, quarter, landed, sems)

        here = slice(chunk * tall, (chunk + 1) * tall)
        pair0 = x_ref[0, here]
        bend0 = jnp.tanh(contract(mix_ref[0], pair0, 1, 0) + bias_ref[0])
        pair1 = (bend0 + pair0.astype(F32)).astype(BF16)
        bend1 = jnp.tanh(contract(mix_ref[1], pair1, 1, 0) + bias_ref[1])
        grad2 = grad_mean(1, chunk)
        gz1 = (grad2 * (1.0 - bend1 * bend1)).astype(BF16)
        gw_ref[1] += contract(pair1, gz1, 1, 1)
        wide1 = gz1.astype(F32)
        gb_ref[1] += jnp.sum(wide1.reshape(each, width, electrons), axis=0)
        grad1 = grad2 + contract(mix_back_ref[1], gz1, 1, 0) + grad_mean(0, chunk)
        gz0 = (grad1 * (1.0 - bend0 * bend0)).astype(BF16)
        gw_ref[0] += contract(pair0, gz0, 1, 1)
        gb_ref[0] += jnp.sum(gz0.astype(F32).reshape(each, width, electrons), axis=0)

    @pl.when(walker == pl.num_programs(0) - 1)
    def _():
        reduce_phase(6, far, feat_ref, gathered, half, quarter, landed, sems)
        sum_ref[...] = gathered[...]


def pair_backward(
    own_spins,
    pair,
    mask_pairs,
    row_parts,
    col_all,
    mix,
    mix_back,
    bias_tall,
    feats,
    width,
    size,
    collective_id,
):
    far = size // 4
    total, lanes = feats.shape
    padded = -(-total // (8 * size)) * 8 * size
    rows = padded // size
    shape = (far, 2, 2, rows, lanes)
    feats = jnp.pad(feats, ((0, padded - total), (0, 0))).reshape(shape)
    walkers, tall_all, electrons = pair.shape
    tall = mix.shape[1]
    gw, gb, sums = pl.pallas_call(
        functools.partial(backward_kernel, width, tall_all // tall, far, walkers),
        grid=(walkers,),
        out_shape=(
            jax.ShapeDtypeStruct((2, tall, tall), F32),
            jax.ShapeDtypeStruct((2, width, electrons), F32),
            jax.ShapeDtypeStruct(shape, F32),
        ),
        in_specs=[
            pl.BlockSpec(memory_space=pltpu.SMEM),
            pl.BlockSpec((1, tall_all, electrons), lambda w: (w, 0, 0)),
            pl.BlockSpec((1,) + mask_pairs.shape[1:], lambda w: (w, 0, 0, 0)),
            pl.BlockSpec((1, 8, tall_all), lambda w: (w, 0, 0)),
            pl.BlockSpec((2, 1, electrons, 4 * width), lambda w: (0, w // 2, 0, 0)),
            pl.BlockSpec(mix.shape, lambda w: (0, 0, 0)),
            pl.BlockSpec(mix.shape, lambda w: (0, 0, 0)),
            pl.BlockSpec(bias_tall.shape, lambda w: (0, 0, 0)),
            pl.BlockSpec(memory_space=pltpu.VMEM),
        ],
        out_specs=(
            pl.BlockSpec((2, tall, tall), lambda w: (0, 0, 0)),
            pl.BlockSpec((2, width, electrons), lambda w: (0, 0, 0)),
            pl.BlockSpec(memory_space=pltpu.VMEM),
        ),
        scratch_shapes=[
            pltpu.VMEM((2, 4, width, electrons), F32),
            pltpu.VMEM((far, 2, rows, lanes), F32),
            pltpu.VMEM((far, rows, lanes), F32),
            pltpu.VMEM((far, rows, lanes), F32),
            pltpu.VMEM(shape, F32),
        ]
        + dma((1,), (1,), (1,), (1,), (far,), (far,), (far,), (far,), (1,), (1,), (1,), (1,)),
        compiler_params=pltpu.CompilerParams(
            vmem_limit_bytes=VMEM_LIMIT, collective_id=collective_id, has_side_effects=True
        ),
    )(own_spins, pair, mask_pairs, row_parts, col_all, mix, mix_back, bias_tall, feats)
    return gw, gb, sums.reshape(padded, lanes)


def general(
    size,
    one_input,
    pair_input,
    spins,
    cotangent,
    w_self,
    w_means,
    w_rows,
    w_cols,
    b_one,
    w_pair,
    b_pair,
):
    highest = lax.Precision.HIGHEST
    walkers, rows_dev, one_width = one_input.shape
    width = pair_input.shape[2]
    electrons = pair_input.shape[3]
    layers = w_self.shape[0]
    flat = walkers * rows_dev
    tall_all = rows_dev * width
    each = math.gcd(rows_dev, 8)
    tall = each * width
    row_start = lax.axis_index("row") * rows_dev

    up_mask = (spins == 1).astype(F32)
    masks = jnp.stack([up_mask, 1.0 - up_mask], axis=1)
    counts = jnp.sum(masks, axis=2)
    own_spins = lax.dynamic_slice_in_dim((spins == 1).astype(jnp.int32), row_start, rows_dev, 1)
    own_mask = lax.dynamic_slice_in_dim(masks, row_start, rows_dev, 2)
    own_up = own_mask[:, 0, :, None] > 0.5

    eye = jnp.eye(each, dtype=BF16)
    mix = jnp.stack([jnp.kron(eye, w_pair[k].T) for k in range(layers - 1)])
    mix_back = jnp.stack([jnp.kron(eye, w_pair[k]) for k in range(layers - 1)])
    bias_tall = jnp.tile(b_pair, (1, each))[:, :, None]
    mask_rows = jnp.pad(masks, ((0, 0), (0, 14), (0, 0))).astype(BF16)
    own_rows = jnp.pad(jnp.repeat(own_mask, width, axis=2), ((0, 0), (0, 6), (0, 0)))
    pair_flat = pair_input.reshape(walkers, tall_all, electrons)

    row_sums, col_part = pair_forward(pair_flat, mask_rows, own_rows, mix, bias_tall, width)
    sum_parts = 2 * layers
    col_part = col_part.reshape(sum_parts, walkers // 4, size, rows_dev, 4 * width)
    col_part = jnp.transpose(col_part, (0, 2, 1, 3, 4)).reshape(sum_parts, size, -1, 4 * width)
    walker_eye = jnp.eye(walkers, dtype=F32)
    gather_mask = (walker_eye[:, None, :, None] * own_mask[:, :, None, :]).reshape(
        2 * walkers, flat
    )
    gather_mask = gather_mask.astype(BF16)
    one_cur = one_input.reshape(flat, one_width)
    first_part = jnp.dot(gather_mask, one_cur, preferred_element_type=F32)
    col_sums, first_sums = reduce_scatter(col_part, first_part, size, 0)
    col_sums = col_sums.reshape(layers, walkers // 2, rows_dev, 2, 2 * width)
    col_sums = jnp.transpose(col_sums, (0, 1, 3, 2, 4)).reshape(
        layers, walkers, rows_dev, 2, width
    )
    row_sums = jnp.transpose(
        row_sums[:, :, :2].reshape(walkers, layers, 2, rows_dev, width), (1, 0, 3, 2, 4)
    )
    scale = counts[None, :, None, :, None]
    row_means = (row_sums / scale).astype(BF16).reshape(layers, flat, 2 * width)
    col_means = (col_sums / scale).astype(BF16).reshape(layers, flat, 2 * width)

    w_all = jnp.concatenate([w_self, w_rows, w_cols], axis=1)
    counts_flat = counts.reshape(2 * walkers, 1)

    stored = []
    for layer in range(layers):
        if layer == 0:
            one_sums = first_sums
        else:
            part_one = jnp.dot(gather_mask, one_cur, preferred_element_type=F32)
            one_sums = reduce_small(part_one, size, 1 + layer)
        one_means = (one_sums / counts_flat).astype(BF16).reshape(walkers, 2 * one_width)
        feats = jnp.concatenate([one_cur, row_means[layer], col_means[layer]], axis=1)
        shared = jnp.dot(one_means, w_means[layer], preferred_element_type=F32) + b_one[layer]
        preact = jnp.dot(feats, w_all[layer], preferred_element_type=F32)
        preact = preact.reshape(walkers, rows_dev, one_width) + shared[:, None, :]
        activation = jnp.tanh(preact)
        stored.append((feats, one_means, activation))
        one_cur = (activation + one_cur.reshape(preact.shape).astype(F32)).astype(BF16)
        one_cur = one_cur.reshape(flat, one_width)
    one_output = one_cur.reshape(walkers, rows_dev, one_width)

    grad_one = cotangent
    feat_grads = [None] * layers
    pre_totals = [None] * layers
    row_parts = []
    col_parts = []
    for layer in reversed(range(layers)):
        feats, one_means, activation = stored[layer]
        grad_pre = (grad_one * (1.0 - activation * activation)).astype(BF16)
        pre_sums = jnp.sum(grad_pre.astype(F32), axis=1)
        flat_pre = grad_pre.reshape(flat, one_width)
        feat_grads[layer] = lax.dot_general(
            feats, flat_pre, (((0,), (0,)), ((), ())), preferred_element_type=F32
        )
        if layer == 0:
            pre_totals[0] = pre_sums
            break
        grad_feat = lax.dot_general(
            flat_pre, w_all[layer], (((1,), (1,)), ((), ())), preferred_element_type=F32
        ).reshape(walkers, rows_dev, one_width + 4 * width)
        side_scale = counts[:, None, :, None]
        row_grad = grad_feat[:, :, one_width : one_width + 2 * width]
        row_grad = row_grad.reshape(walkers, rows_dev, 2, width) / side_scale
        row_parts.append(jnp.transpose(row_grad, (0, 2, 1, 3)).reshape(walkers, 2, tall_all))
        col_grad = grad_feat[:, :, one_width + 2 * width :]
        col_grad = (col_grad.reshape(walkers, rows_dev, 2, width) / side_scale).reshape(
            walkers // 2, 2, rows_dev, 2 * width
        )
        col_parts.append(jnp.transpose(col_grad, (0, 2, 1, 3)).reshape(-1, 4 * width))
        if layer == 1:
            col_all, pre_totals[layer] = all_gather(
                jnp.concatenate([col_parts[1], col_parts[0]]).reshape(4, -1, 4 * width),
                pre_sums,
                size,
                2 + 2 * layers,
            )
        else:
            pre_totals[layer] = reduce_small(pre_sums, size, 1 + layers + layer)
        mean_total = jnp.einsum(
            "wh,ah->wa", pre_totals[layer], w_means[layer].astype(F32), precision=highest
        )
        mean_total = mean_total.reshape(walkers, 2, one_width) / counts[:, :, None]
        grad_one = (
            grad_one
            + grad_feat[:, :, :one_width]
            + jnp.where(own_up, mean_total[:, None, 0], mean_total[:, None, 1])
        )

    row_stack = jnp.concatenate(
        [row_parts[1], row_parts[0], jnp.zeros((walkers, 4, tall_all), F32)], axis=1
    )
    col_all = col_all.reshape(4, size, walkers // 4, rows_dev, 4 * width)
    col_all = jnp.transpose(col_all, (0, 2, 1, 3, 4)).reshape(
        2, walkers // 2, electrons, 4 * width
    )
    lower = jnp.pad(masks, ((0, 0), (0, 6), (0, 0)))
    upper = jnp.pad(masks, ((0, 0), (2, 4), (0, 0)))
    mask_pairs = jnp.stack(
        [
            jnp.concatenate([piece, piece, piece, jnp.zeros_like(piece)], axis=1)
            for piece in (lower, upper)
        ],
        axis=1,
    ).astype(BF16)
    gw, gb, feat_sums = pair_backward(
        own_spins,
        pair_flat,
        mask_pairs,
        row_stack,
        col_all,
        mix,
        mix_back,
        bias_tall,
        jnp.concatenate(feat_grads, axis=0),
        width,
        size,
        3 + 2 * layers,
    )
    g_wpair = jnp.einsum("lacad->lcd", gw.reshape(layers - 1, each, width, each, width))
    g_bpair = jnp.sum(gb, axis=2)

    tail = jnp.concatenate([g_wpair.reshape(-1), g_bpair.reshape(-1)])
    unit = 8 * one_width
    tail = jnp.pad(tail, (0, -tail.size % unit)).reshape(-1, one_width)
    ends = reduce_small(jnp.concatenate([pre_totals[0], tail], axis=0), size, 4 + 2 * layers)
    deep = one_width + 4 * width
    first = feat_sums[: layers * deep].reshape(layers, deep, one_width)
    pre_totals[0] = ends[:walkers]
    tail = ends[walkers:].reshape(-1)
    square = width * width
    pre_all = jnp.stack(pre_totals)
    means_all = jnp.stack([item[1] for item in stored]).astype(F32)
    grad_means = jnp.einsum("lwa,lwk->lak", means_all, pre_all, precision=highest)
    count = layers - 1
    return (
        one_output,
        first[:, :one_width],
        grad_means,
        first[:, one_width : one_width + 2 * width],
        first[:, one_width + 2 * width :],
        jnp.sum(pre_all, axis=1),
        tail[: count * square].reshape(count, width, width),
        tail[count * square : count * square + count * width].reshape(count, width),
    )


def iota(shape, dim):
    return lax.broadcasted_iota(jnp.int32, shape, dim)


def split3(x):
    high = x.astype(BF16).astype(F32)
    rest = x - high
    mid = rest.astype(BF16).astype(F32)
    return jnp.concatenate([high, mid, rest - mid], axis=0).astype(BF16)


class Place:
    def __init__(self, far):
        self.far = far
        self.me, self.core, self.side, self.high = position()
        self.low = lax.rem(self.me, 4)
        self.peer_core = self.me + 1 - 2 * self.core
        self.peer_side = self.me + 2 - 4 * self.side
        self.far_ids = [
            (d, lax.rem(self.high + d + 1, far), lax.rem(self.high + d + 1, far) * 4 + self.low)
            for d in range(far - 1)
        ]
        self.near_ids = [(d, self.high * 4 + lax.rem(self.low + d + 1, 4)) for d in range(3)]


def remote(src, dst, send_sem, recv_sem, target):
    return pltpu.make_async_remote_copy(
        src_ref=src,
        dst_ref=dst,
        send_sem=send_sem,
        recv_sem=recv_sem,
        device_id={"row": target},
        device_id_type=MESH,
    )


class SmallSum:
    def __init__(self, place, across, within, sems):
        self.place, self.across, self.within = place, across, within
        self.sems = sems

    def far_copies(self, k):
        sf, rf, _, _ = self.sems
        mine = self.across.at[k, self.place.high]
        return [
            remote(mine, mine, sf.at[k, d], rf.at[k, d], target)
            for d, _, target in self.place.far_ids
        ]

    def near_copies(self, k):
        _, _, sn, rn = self.sems
        mine = self.within.at[k, self.place.low]
        return [
            remote(mine, mine, sn.at[k, d], rn.at[k, d], target)
            for d, target in self.place.near_ids
        ]

    def start(self, k, value):
        self.across[k, self.place.high] = value
        for copy in self.far_copies(k):
            copy.start()

    def middle(self, k):
        for copy in self.far_copies(k):
            copy.wait()
        total = self.across[k, 0]
        for n in range(1, self.place.far):
            total = total + self.across[k, n]
        self.within[k, self.place.low] = total
        for copy in self.near_copies(k):
            copy.start()

    def finish(self, k):
        for copy in self.near_copies(k):
            copy.wait()
        total = self.within[k, 0]
        for n in range(1, 4):
            total = total + self.within[k, n]
        return total


class ColumnSums:
    def __init__(self, place, source, half, quarter, landed, total, sems):
        self.place, self.source, self.half, self.quarter = place, source, half, quarter
        self.landed, self.total, self.sems = landed, total, sems

    def first(self, k):
        sa, ra = self.sems[0:2]
        p = self.place
        return remote(
            self.source.at[k, :, :, 1 - p.core], self.half.at[k], sa.at[k], ra.at[k], p.peer_core
        )

    def second(self, k):
        sb, rb = self.sems[2:4]
        p = self.place
        return remote(
            self.half.at[k, :, 1 - p.side], self.quarter.at[k], sb.at[k], rb.at[k], p.peer_side
        )

    def third(self, k):
        sc, rc = self.sems[4:6]
        return [
            remote(
                self.quarter.at[k, z], self.landed.at[k, d], sc.at[k, d], rc.at[k, d], target
            )
            for d, z, target in self.place.far_ids
        ]

    def a(self, k):
        self.first(k).start()

    def b(self, k):
        self.first(k).wait()
        self.half[k] = self.half[k] + self.source[k, :, :, self.place.core]
        self.second(k).start()

    def c(self, k):
        self.second(k).wait()
        self.quarter[k] = self.quarter[k] + self.half[k, :, self.place.side]
        for copy in self.third(k):
            copy.start()

    def d(self, k):
        for copy in self.third(k):
            copy.wait()
        total = self.quarter[k, self.place.high]
        for n in range(self.place.far - 1):
            total = total + self.landed[k, n]
        self.total[k] = total


class Gather:
    def __init__(self, place, ref, sems):
        self.place, self.ref, self.sems = place, ref, sems

    def far_copies(self, k):
        p = self.place
        sa, ra = self.sems[0:2]
        mine = self.ref.at[k, p.high, p.side, p.core]
        return [remote(mine, mine, sa.at[k, d], ra.at[k, d], target) for d, _, target in p.far_ids]

    def side_copies(self, k):
        p = self.place
        sb, rb = self.sems[2:4]
        got = []
        for d in range(p.far):
            block = self.ref.at[k, lax.rem(p.high - d - 1 + p.far, p.far), p.side, p.core]
            got.append(remote(block, block, sb.at[k, d], rb.at[k, d], p.peer_side))
        return got

    def core_copy(self, k):
        p = self.place
        sc, rc = self.sems[4:6]
        block = self.ref.at[k, :, :, p.core]
        return remote(block, block, sc.at[k], rc.at[k], p.peer_core)

    def step(self, k, phase):
        if phase == 0:
            for copy in self.far_copies(k):
                copy.start()
            self.side_copies(k)[-1].start()
        elif phase == 1:
            onward = self.side_copies(k)
            for d, copy in enumerate(self.far_copies(k)):
                copy.wait()
                onward[d].start()
        elif phase == 2:
            for copy in self.side_copies(k):
                copy.wait()
            self.core_copy(k).start()
        else:
            self.core_copy(k).wait()


def whole_kernel(
    dims,
    one_ref,
    pair_hbm,
    spins_ref,
    cot_ref,
    wself_ref,
    wmeans_ref,
    wrows_ref,
    wcols_ref,
    bone_ref,
    wpair_ref,
    bpair_ref,
    oneout_ref,
    feat_all,
    means,
    pre_all,
    gtail_ref,
    pair0,
    pair1,
    slope0,
    slope1,
    mask16,
    sel,
    mix,
    mix_back,
    bias,
    wbig,
    gmask,
    upcol,
    coef,
    cg,
    cnt_y,
    ysum,
    feats,
    act,
    grad_one,
    col_two,
    rhs,
    gw,
    cs_source,
    cs_half,
    cs_quarter,
    cs_landed,
    cs_total,
    ag_ref,
    fs_across,
    fs_within,
    bs_across,
    bs_within,
    es_across,
    es_within,
    feat_ref,
    feat_half,
    feat_quarter,
    feat_landed,
    load_sem,
    again_sem,
    *sems,
):
    walkers, rows, width, electrons, one_width, layers, far, tall = dims
    flat = walkers * rows
    tall_all = rows * width
    chunks = tall_all // tall
    each = tall // width
    pairs = walkers // 2
    place = Place(far)

    loads = [
        pltpu.make_async_copy(pair_hbm.at[w], pair0.at[w], load_sem.at[w]) for w in range(walkers)
    ]
    for load in loads:
        load.start()
    again = [
        pltpu.make_async_copy(pair_hbm.at[w], pair0.at[w], again_sem.at[w]) for w in range(walkers)
    ]

    barrier = pltpu.get_barrier_semaphore()
    peers = [t for _, _, t in place.far_ids] + [t for _, t in place.near_ids]
    for target in peers:
        pl.semaphore_signal(barrier, inc=1, device_id={"row": target}, device_id_type=MESH)

    sems = list(sems)

    def take(n):
        got = sems[:n]
        del sems[:n]
        return got

    columns = ColumnSums(place, cs_source, cs_half, cs_quarter, cs_landed, cs_total, take(6))
    gather = Gather(place, ag_ref, take(6))
    fwd_sum = SmallSum(place, fs_across, fs_within, take(4))
    bwd_sum = SmallSum(place, bs_across, bs_within, take(4))
    end_sum = SmallSum(place, es_across, es_within, take(4))
    feat_sems = take(12)

    up = (spins_ref[...] == 1).astype(F32)
    down = 1.0 - up
    count_up = jnp.sum(up, axis=1, keepdims=True)
    count_down = jnp.sum(down, axis=1, keepdims=True)
    counts16 = jnp.concatenate([count_up, count_down], axis=0)
    both_spins = jnp.concatenate([up, down], axis=0).astype(BF16)
    first_row = place.me * rows

    pick = (iota((electrons, flat), 0) == first_row + lax.rem(iota((electrons, flat), 1), rows))
    own = contract(both_spins, pick.astype(BF16), 1, 0)
    same = lax.rem(iota((2 * walkers, flat), 0), walkers) == iota((2 * walkers, flat), 1) // rows
    gmask[...] = jnp.where(same, own, 0.0).astype(BF16)
    fwd_partial = contract(gmask[...], one_ref[...], 1, 0)
    pl.semaphore_wait(barrier, len(peers))
    fwd_sum.start(0, fwd_partial)

    lane = iota((width, tall), 1)
    eye_tall = (lax.rem(iota((tall, width), 0), width) == iota((tall, width), 1)).astype(BF16)
    same_block = iota((tall, tall), 0) // width == iota((tall, tall), 1) // width
    for k in range(layers - 1):
        for target, dim in ((mix, 1), (mix_back, 0)):
            part = contract(eye_tall, wpair_ref[k], 1, dim).astype(BF16)
            full = contract(part, eye_tall, 1, 1)
            target[k] = jnp.where(same_block, full, 0.0).astype(BF16)
        bias[k] = jnp.sum(eye_tall.astype(F32) * bpair_ref[k : k + 1, :], axis=1, keepdims=True)

    spread = iota((electrons, tall_all), 0) == first_row + iota((electrons, tall_all), 1) // width
    own_rows = contract(both_spins, spread.astype(BF16), 1, 0)
    eye_wide = (lax.rem(iota((width, tall_all), 1), width) == iota((width, tall_all), 0)).astype(F32)
    row_id = iota((16, electrons), 0)
    for w in range(walkers):
        mask16[w] = jnp.where(
            row_id == 0, up[w : w + 1], jnp.where(row_id == 1, down[w : w + 1], 0.0)
        ).astype(BF16)
        sel[w] = jnp.concatenate(
            [eye_wide * own_rows[w : w + 1], eye_wide * own_rows[walkers + w : walkers + w + 1]],
            axis=0,
        ).astype(BF16)

    def walker_counts(w, lanes, period):
        is_up = lax.rem(iota((1, lanes), 1), 2 * period) < period
        return jnp.where(is_up, count_up[w : w + 1], count_down[w : w + 1])

    for w in range(walkers):
        cg[w] = jnp.broadcast_to(walker_counts(w, 4 * width, width), (rows, 4 * width))
        cnt_y[w] = jnp.broadcast_to(walker_counts(w, 8 * width, 4 * width), (8, 8 * width))
    which = lax.rem(iota((2 * walkers, 4 * width), 1), 2 * width) // width
    chooser = (iota((2 * walkers, 4 * width), 0) // walkers == which).astype(BF16)
    own_cols = contract(gmask[...], chooser, 0, 0)
    for level in range(2):
        coef[level, :, 4 * width :] = own_cols
    is_up_row = (iota((2 * walkers, one_width), 0) < walkers).astype(BF16)
    upcol[...] = contract(gmask[...], is_up_row, 0, 0)
    for k in range(layers):
        wbig[k, :one_width] = wself_ref[k]
        for start, ref in ((0, wrows_ref), (4, wcols_ref)):
            for copy in range(2):
                low = one_width + (start + 2 * copy) * width
                wbig[k, low : low + 2 * width] = ref[k]

    def row_sums(layer, w, chunk, pair):
        got = contract(mask16[w], pair, 1, 1)
        for k in range(tall // 128):
            for s in range(2):
                ysum[layer, w, pl.ds(chunk * (tall // 128) + k, 1), s * 128 : (s + 1) * 128] = got[
                    s : s + 1, k * 128 : (k + 1) * 128
                ]

    def stream(layer, w, slot, source, source_w, slopes, target, target_w):
        cols = None
        for chunk in range(chunks):
            here = slice(chunk * tall, (chunk + 1) * tall)
            pair = source[source_w, here]
            row_sums(layer, w, chunk, pair)
            left = jnp.concatenate([mix[layer], sel[w, :, here]], axis=0)
            both = contract(left, pair, 1, 0)
            part = both[tall:]
            cols = part if cols is None else cols + part
            bend = jnp.tanh(both[:tall] + bias[layer])
            slopes[w, here] = (1.0 - bend * bend).astype(BF16)
            target[target_w, here] = (bend + pair.astype(F32)).astype(BF16)
        col_two[slot] = cols

    def sums_only(layer, w, slot):
        cols = None
        for chunk in range(chunks):
            here = slice(chunk * tall, (chunk + 1) * tall)
            pair = pair0[w, here]
            row_sums(layer, w, chunk, pair)
            part = contract(sel[w, :, here], pair, 1, 0)
            cols = part if cols is None else cols + part
        col_two[slot] = cols

    lags = ((1, columns.b), (4, columns.c), (7, columns.d))

    def tick(t):
        both = col_two[...].reshape(4 * width, electrons)
        cs_source[t] = both.T.reshape(far, 2, 2, rows, 4 * width)
        columns.a(t)
        for lag, step in lags:

            @pl.when(t >= lag)
            def _(lag=lag, step=step):
                step(t - lag)

    def part_of(layer, p):
        return layer * pairs + p

    def one_layer(layer):
        totals = fwd_sum.finish(layer)
        mean = (totals / counts16).astype(BF16)
        means[layer] = mean
        ups = contract(mean, wmeans_ref[layer, :one_width], 1, 0)
        downs = contract(mean, wmeans_ref[layer, one_width:], 1, 0)
        shared = ups[:walkers] + downs[walkers:] + bone_ref[layer : layer + 1, :]
        lanes = 8 * width
        ys = (ysum[layer] / cnt_y[...]).reshape(walkers * 8, lanes).astype(BF16)
        per = rows // 8
        expand = iota((flat, walkers * 8), 0) // per == iota((flat, walkers * 8), 1)
        wide = contract(expand.astype(BF16), ys, 1, 0)
        keep = lax.rem(iota((flat, lanes), 1) // width, 4) == lax.rem(iota((flat, lanes), 0), per)
        wide = jnp.where(keep, wide, 0.0).astype(BF16)
        src, dst = iota((lanes, 4 * width), 0), iota((lanes, 4 * width), 1)
        fold = (src // (4 * width)) * width + lax.rem(src, width) == dst
        row_mean = contract(wide, fold.astype(BF16), 1, 0)
        first_half = iota((rows, 4 * width), 1) < 2 * width
        col_mean = []
        for p in range(pairs):
            total = cs_total[part_of(layer, p)]
            col_mean.append(jnp.where(first_half, total / cg[2 * p], 0.0))
            col_mean.append(jnp.where(first_half, 0.0, total / cg[2 * p + 1]))
        current = one_ref[...] if layer == 0 else oneout_ref[...]
        feats[layer, :, :one_width] = current
        feats[layer, :, one_width : one_width + 4 * width] = row_mean.astype(BF16)
        feats[layer, :, one_width + 4 * width :] = jnp.concatenate(col_mean, axis=0).astype(BF16)
        preact = contract(feats[layer], wbig[layer], 1, 0)
        for w in range(walkers):
            here = slice(w * rows, (w + 1) * rows)
            bend = jnp.tanh(preact[here] + shared[w : w + 1])
            act[layer, here] = bend
            oneout_ref[here] = (bend + current[here].astype(F32)).astype(BF16)
        if layer + 1 < layers:
            fwd_sum.start(layer + 1, contract(gmask[...], oneout_ref[...], 1, 0))

    def load_wait(w):
        for k in range(walkers):

            @pl.when(w == k)
            def _(k=k):
                loads[k].wait()

    def pass0(p, carry):
        def body(slot, inner):
            w = 2 * p + slot
            load_wait(w)
            stream(0, w, slot, pair0, w, slope0, pair1, w)
            return inner

        lax.fori_loop(0, 2, body, 0)
        tick(p)

        @pl.when(p == 1)
        def _():
            fwd_sum.middle(0)

        return carry

    lax.fori_loop(0, pairs, pass0, 0)

    def pass1(p, carry):
        def body(slot, inner):
            w = 2 * p + slot
            stream(1, w, slot, pair1, w, slope1, pair0, w)
            return inner

        lax.fori_loop(0, 2, body, 0)
        tick(pairs + p)
        return carry

    lax.fori_loop(0, pairs, pass1, 0)

    def pass2(p, carry):
        def body(slot, inner):
            sums_only(2, 2 * p + slot, slot)
            return inner

        lax.fori_loop(0, 2, body, 0)
        tick(2 * pairs + p)

        @pl.when(p == 2)
        def _():
            one_layer(0)

        return carry

    lax.fori_loop(0, pairs, pass2, 0)
    for load in again:
        load.start()
    columns.b(11)
    columns.c(8)
    columns.d(5)
    columns.c(9)
    fwd_sum.middle(1)
    columns.d(6)
    columns.c(10)
    columns.d(7)
    columns.c(11)
    one_layer(1)
    columns.d(8)
    columns.d(9)
    fwd_sum.middle(2)
    columns.d(10)
    columns.d(11)
    one_layer(2)

    walker_sum = (iota((16, flat), 0) == iota((16, flat), 1) // rows).astype(BF16)
    blocks = 4 * far
    deep = one_width + 4 * width
    block_rows = deep // blocks

    def cotangents(layer, level):
        grad = cot_ref[...] if layer == layers - 1 else grad_one[...]
        bend = act[layer]
        pre = (grad * (1.0 - bend * bend)).astype(BF16)
        index = layers - 1 - layer
        bwd_sum.start(index, contract(walker_sum, pre, 1, 0)[:walkers])
        if layer > 0:
            back = contract(pre, wbig[layer], 1, 1)
            grad_one[...] = grad + back[:, :one_width]
            counts = cg[...].reshape(flat, 4 * width)
            col = back[:, one_width + 4 * width :] / counts
            first_half = iota((rows, 4 * width), 1) < 2 * width
            for p in range(pairs):
                even = col[2 * p * rows : (2 * p + 1) * rows]
                odd = col[(2 * p + 1) * rows : (2 * p + 2) * rows]
                ag_ref[level, place.high, place.side, place.core, p] = jnp.where(
                    first_half, even, odd
                )
            gather.step(level, 0)
            row = back[:, one_width : one_width + 4 * width] / counts
            if layer < layers - 1:
                row = row + coef[1 - level, :, : 4 * width]
            coef[level, :, : 4 * width] = row
        grads = contract(feats[layer], pre, 0, 0)
        cols_at = one_width + 4 * width
        kept = jnp.concatenate(
            [
                grads[: one_width + 2 * width],
                grads[cols_at : cols_at + 2 * width] + grads[cols_at + 2 * width :],
            ],
            axis=0,
        )
        for b in range(blocks):
            feat_ref[layer, b // 4, (b // 2) % 2, b % 2] = kept[b * block_rows : (b + 1) * block_rows]

    def finish_pre(layer):
        total = bwd_sum.finish(layers - 1 - layer)
        pre_all[layer] = total
        return split3(total)

    def feat(layer, phase):
        reduce_phase(
            phase,
            far,
            feat_ref.at[layer],
            feat_all.at[layer],
            feat_half.at[layer],
            feat_quarter.at[layer],
            feat_landed.at[layer],
            [sem.at[layer] for sem in feat_sems],
        )

    def spread_means(layer):
        pieces = finish_pre(layer)
        back = contract(pieces, wmeans_ref[layer], 1, 1)
        total = back[:walkers] + back[walkers : 2 * walkers] + back[2 * walkers :]
        mean_up = total[:, :one_width] / count_up
        mean_down = total[:, one_width:] / count_down
        for w in range(walkers):
            here = slice(w * rows, (w + 1) * rows)
            grad_one[here] = grad_one[here] + jnp.where(
                upcol[here] > 0.5, mean_up[w : w + 1], mean_down[w : w + 1]
            )

    cotangents(2, 0)
    feat(2, 0)
    bwd_sum.middle(0)
    gather.step(0, 1)
    feat(2, 1)
    spread_means(2)
    cotangents(1, 1)
    feat(1, 0)
    bwd_sum.middle(1)
    gather.step(0, 2)
    feat(2, 2)
    spread_means(1)
    cotangents(0, 0)
    feat(0, 0)
    feat(1, 1)
    for load in again:
        load.wait()

    first_half = iota((flat, 4 * width), 1) < 2 * width
    for level in range(2):
        row = coef[level, :, : 4 * width]
        lead = row.astype(BF16).astype(F32)
        coef[level, :, : 4 * width] = jnp.where(first_half, lead, row - lead)

    gw[...] = jnp.zeros_like(gw)
    gather.step(0, 3)

    lane_eye = (
        lax.rem(iota((width, 8 * width), 1), width) == iota((width, 8 * width), 0)
    ).astype(F32)
    ones = jnp.ones((16, electrons), BF16)
    spin_of = lax.rem(iota((4 * width, electrons), 0), 2 * width) < width

    def prepare(level, p):
        turned = []
        for n in range(level + 1):
            block = ag_ref[n, :, :, :, p].reshape(electrons, 4 * width)
            turned.append(block)
        total = turned[0] if level == 0 else turned[0] + turned[1]
        total = total.T
        for slot in range(2):
            mine = total[slot * 2 * width : (slot + 1) * 2 * width]
            lead = mine.astype(BF16)
            rhs[slot, 4 * width : 6 * width] = lead
            rhs[slot, 6 * width :] = (mine - lead.astype(F32)).astype(BF16)
            spins = mask16[2 * p + slot].astype(F32)
            rhs[slot, : 4 * width] = jnp.where(spin_of, spins[0:1], spins[1:2]).astype(BF16)

    def spread_coef(level, w, chunk):
        pieces = []
        for e in range(each):
            line = coef[level, pl.ds(w * rows + chunk * each + e, 1), :]
            pieces.append(lane_eye * line)
        return jnp.concatenate(pieces, axis=0).astype(BF16)

    def level_one(p, slot):
        w = 2 * p + slot
        for chunk in range(chunks):
            here = slice(chunk * tall, (chunk + 1) * tall)
            grad = contract(spread_coef(0, w, chunk), rhs[slot], 1, 0)
            gz = (grad * slope1[w, here].astype(F32)).astype(BF16)
            slope1[w, here] = gz
            gw[1] += contract(jnp.concatenate([pair1[w, here], ones], axis=0), gz, 1, 1)

    def level_zero(p, slot):
        w = 2 * p + slot
        for chunk in range(chunks):
            here = slice(chunk * tall, (chunk + 1) * tall)
            left = jnp.concatenate([mix_back[1], spread_coef(1, w, chunk)], axis=1)
            right = jnp.concatenate([slope1[w, here], rhs[slot]], axis=0)
            grad = contract(left, right, 1, 0)
            gz = (grad * slope0[w, here].astype(F32)).astype(BF16)
            gw[0] += contract(jnp.concatenate([pair0[w, here], ones], axis=0), gz, 1, 1)

    def run(level, work, after):
        def step(p, carry):
            prepare(level, p)

            def body(slot, inner):
                work(p, slot)
                for at, todo in after:

                    @pl.when(2 * p + slot == at)
                    def _(todo=todo):
                        todo()

                return inner

            lax.fori_loop(0, 2, body, 0)
            return carry

        lax.fori_loop(0, pairs, step, 0)

    def at(step, work, *args):
        return step, lambda: work(*args)

    run(
        0,
        level_one,
        [
            at(0, feat, 0, 1),
            at(1, gather.step, 1, 1),
            at(1, bwd_sum.middle, 2),
            at(2, feat, 2, 3),
            at(3, feat, 1, 2),
            at(4, gather.step, 1, 2),
            at(5, feat, 0, 2),
            at(5, finish_pre, 0),
            at(6, feat, 2, 4),
            at(7, feat, 1, 3),
        ],
    )
    gather.step(1, 3)
    run(
        1,
        level_zero,
        [
            at(0, feat, 0, 3),
            at(1, feat, 2, 5),
            at(2, feat, 1, 4),
            at(3, feat, 0, 4),
            at(4, feat, 2, 6),
            at(5, feat, 1, 5),
            at(6, feat, 0, 5),
        ],
    )

    lanes_total = None
    for k in range(layers - 1):
        grid = gw[k]
        folded = jnp.zeros((width, tall), F32)
        for a in range(each):
            folded = folded + jnp.where(
                lane // width == a, grid[a * width : (a + 1) * width], 0.0
            )
        folded = jnp.concatenate([folded, grid[tall : tall + 8]], axis=0)
        src, dst = iota((tall, 128), 0), iota((tall, 128), 1)
        fold = (lax.rem(src, width) + k * width == dst).astype(BF16)
        pieces = contract(split3(folded), fold, 1, 0)
        size = width + 8
        piece = pieces[:size] + pieces[size : 2 * size] + pieces[2 * size :]
        lanes_total = piece if lanes_total is None else lanes_total + piece
    end_sum.start(0, lanes_total)
    feat(1, 6)
    feat(0, 6)
    end_sum.middle(0)
    gtail_ref[...] = end_sum.finish(0)


def ends_kernel(
    dims,
    one_ref,
    feat_all,
    means,
    pre_all,
    tail,
    oneout_ref,
    gself_ref,
    gmeans_ref,
    grows_ref,
    gcols_ref,
    gbias_ref,
    gwpair_ref,
    gbpair_ref,
    gself,
    gmeans,
    grows,
    gcols,
    gbias,
    gwpair,
    gbpair,
    sem,
):
    walkers, width, one_width, layers, far = dims
    blocks = 4 * far
    rows = feat_all.shape[-2]
    edges = [0, one_width, one_width + 2 * width, one_width + 4 * width]
    moves = []

    def move(src, dst):
        copy = pltpu.make_async_copy(src, dst, sem.at[len(moves)])
        copy.start()
        moves.append(copy)

    move(one_ref, oneout_ref)
    for layer in range(layers):
        for b in range(blocks):
            for n, out in enumerate((gself, grows, gcols)):
                low, high = max(edges[n], b * rows), min(edges[n + 1], (b + 1) * rows)
                if low < high:
                    out[layer, low - edges[n] : high - edges[n]] = feat_all[
                        layer, b // 4, (b // 2) % 2, b % 2, low - b * rows : high - b * rows
                    ]
        move(gself.at[layer], gself_ref.at[layer])
    move(grows, grows_ref)
    move(gcols, gcols_ref)
    for layer in range(layers):
        total = pre_all[layer]
        pieces = split3(total)
        mean = means[layer].astype(F32)
        for s in range(2):
            piece = mean[s * walkers : (s + 1) * walkers]
            tripled = jnp.concatenate([piece, piece, piece], axis=0).astype(BF16)
            gmeans[layer, s * one_width : (s + 1) * one_width] = contract(tripled, pieces, 0, 0)
        move(gmeans.at[layer], gmeans_ref.at[layer])
        gbias[layer : layer + 1] = jnp.sum(total, axis=0, keepdims=True)
    for k in range(layers - 1):
        gwpair[k] = tail[:width, k * width : (k + 1) * width]
        gbpair[k : k + 1] = tail[width : width + 1, k * width : (k + 1) * width]
    move(gbias, gbias_ref)
    move(gwpair, gwpair_ref)
    move(gbpair, gbpair_ref)
    for copy in moves:
        copy.wait()


def local(
    size,
    one_input,
    pair_input,
    spins,
    cotangent,
    w_self,
    w_means,
    w_rows,
    w_cols,
    b_one,
    w_pair,
    b_pair,
):
    walkers, rows, one_width = one_input.shape
    width, electrons = pair_input.shape[2:]
    layers = w_self.shape[0]
    far = size // 4
    if rows * width != 1024 or width != 32 or walkers != 8 or layers != 3 or far < 2:
        return general(
            size,
            one_input,
            pair_input,
            spins,
            cotangent,
            w_self,
            w_means,
            w_rows,
            w_cols,
            b_one,
            w_pair,
            b_pair,
        )
    flat = walkers * rows
    tall_all = rows * width
    tall = 8 * width
    pairs = walkers // 2
    parts = layers * pairs
    deep = one_width + 4 * width
    block = deep // size
    lanes = 4 * width
    dims = (walkers, rows, width, electrons, one_width, layers, far, tall)
    vmem = pltpu.VMEM
    scratch = [
        vmem((walkers, tall_all, electrons), BF16),
        vmem((walkers, tall_all, electrons), BF16),
        vmem((walkers, tall_all, electrons), BF16),
        vmem((walkers, tall_all, electrons), BF16),
        vmem((walkers, 16, electrons), BF16),
        vmem((walkers, 2 * width, tall_all), BF16),
        vmem((layers - 1, tall, tall), BF16),
        vmem((layers - 1, tall, tall), BF16),
        vmem((layers - 1, tall, 1), F32),
        vmem((layers, one_width + 2 * lanes, one_width), BF16),
        vmem((2 * walkers, flat), BF16),
        vmem((flat, one_width), F32),
        vmem((2, flat, 2 * lanes), F32),
        vmem((walkers, rows, lanes), F32),
        vmem((walkers, 8, 2 * lanes), F32),
        vmem((layers, walkers, 8, 2 * lanes), F32),
        vmem((layers, flat, one_width + 2 * lanes), BF16),
        vmem((layers, flat, one_width), F32),
        vmem((flat, one_width), F32),
        vmem((2, 2 * width, electrons), F32),
        vmem((2, 2 * lanes, electrons), BF16),
        vmem((2, tall + 16, tall), F32),
        vmem((parts, far, 2, 2, rows, lanes), F32),
        vmem((parts, far, 2, rows, lanes), F32),
        vmem((parts, far, rows, lanes), F32),
        vmem((parts, far - 1, rows, lanes), F32),
        vmem((parts, rows, lanes), F32),
        vmem((2, far, 2, 2, pairs, rows, lanes), F32),
        vmem((layers, far, 2 * walkers, one_width), F32),
        vmem((layers, 4, 2 * walkers, one_width), F32),
        vmem((layers, far, walkers, one_width), F32),
        vmem((layers, 4, walkers, one_width), F32),
        vmem((1, far, width + 8, 128), F32),
        vmem((1, 4, width + 8, 128), F32),
        vmem((layers, far, 2, 2, block, one_width), F32),
        vmem((layers, far, 2, block, one_width), F32),
        vmem((layers, far, block, one_width), F32),
        vmem((layers, far, block, one_width), F32),
    ]
    scratch += dma((walkers,), (walkers,))
    scratch += dma((parts,), (parts,), (parts,), (parts,), (parts, far), (parts, far))
    scratch += dma((2, far), (2, far), (2, far), (2, far), (2,), (2,))
    scratch += dma(*([(layers, far), (layers, far), (layers, 4), (layers, 4)] * 2))
    scratch += dma((1, far), (1, far), (1, 4), (1, 4))
    scratch += dma(*[(layers, n) for n in (1, 1, 1, 1, far, far, far, far, 1, 1, 1, 1)])
    in_vmem = pl.BlockSpec(memory_space=pltpu.VMEM)
    shape = jax.ShapeDtypeStruct
    out = pl.pallas_call(
        functools.partial(whole_kernel, dims),
        out_shape=(
            shape((flat, one_width), BF16),
            shape((layers, far, 2, 2, block, one_width), F32),
            shape((layers, 2 * walkers, one_width), BF16),
            shape((layers, walkers, one_width), F32),
            shape((width + 8, 128), F32),
        ),
        in_specs=[in_vmem, pl.BlockSpec(memory_space=pl.ANY)] + [in_vmem] * 9,
        out_specs=(in_vmem,) * 5,
        scratch_shapes=scratch,
        compiler_params=pltpu.CompilerParams(
            vmem_limit_bytes=60 * 1024 * 1024, collective_id=0, has_side_effects=True
        ),
    )(
        one_input.reshape(flat, one_width),
        pair_input.reshape(walkers, tall_all, electrons),
        spins,
        cotangent.reshape(flat, one_width),
        w_self,
        w_means,
        w_rows,
        w_cols,
        b_one,
        w_pair,
        b_pair,
    )
    results = (
        shape((flat, one_width), BF16),
        shape((layers, one_width, one_width), F32),
        shape((layers, 2 * one_width, one_width), F32),
        shape((layers, 2 * width, one_width), F32),
        shape((layers, 2 * width, one_width), F32),
        shape((layers, one_width), F32),
        shape((layers - 1, width, width), F32),
        shape((layers - 1, width), F32),
    )
    anywhere = pl.BlockSpec(memory_space=pl.ANY)
    one_out, *rest = pl.pallas_call(
        functools.partial(ends_kernel, (walkers, width, one_width, layers, far)),
        out_shape=results,
        in_specs=[in_vmem] * 5,
        out_specs=(anywhere,) * len(results),
        scratch_shapes=[vmem(results[n].shape, F32) for n in range(1, 8)]
        + dma((2 * layers + 6,)),
    )(*out)
    return one_out.reshape(walkers, rows, one_width), *rest


def solution(mesh):
    in_specs = (
        P("group", "row", None),
        P("group", "row", None, None),
        P("group", None),
        P("group", "row", None),
        P(),
        P(),
        P(),
        P(),
        P(),
        P(),
        P(),
    )
    out_specs = (
        P("group", "row", None),
        P("group", None, None),
        P("group", None, None),
        P("group", None, None),
        P("group", None, None),
        P("group", None),
        P("group", None, None),
        P("group", None),
    )
    return jax.shard_map(
        functools.partial(local, mesh.shape["row"]),
        mesh=mesh,
        in_specs=in_specs,
        out_specs=out_specs,
        check_vma=False,
    )
```

```python
import functools
import math

import jax
import jax.numpy as jnp
from jax import lax
from jax.experimental import pallas as pl
from jax.experimental.pallas import tpu as pltpu
from jax.sharding import PartitionSpec as P

F32 = jnp.float32
BF16 = jnp.bfloat16
MESH = pl.DeviceIdType.MESH
VMEM_LIMIT = 48 * 1024 * 1024


def greet(targets):
    barrier = pltpu.get_barrier_semaphore()
    for target in targets:
        pl.semaphore_signal(barrier, inc=1, device_id={"row": target}, device_id_type=MESH)
    pl.semaphore_wait(barrier, len(targets))


def send(src, dst, send_sem, recv_sem, target):
    copy = pltpu.make_async_remote_copy(
        src_ref=src,
        dst_ref=dst,
        send_sem=send_sem,
        recv_sem=recv_sem,
        device_id={"row": target},
        device_id_type=MESH,
    )
    copy.start()
    return copy


def neighbours(near, far):
    me = lax.axis_index("row")
    low = lax.rem(me, near)
    high = me // near
    near_ids = [high * near + lax.rem(low + k, near) for k in range(1, near)]
    far_ids = [lax.rem(high + k, far) * near + low for k in range(1, far)]
    return low, high, near_ids, far_ids


def small_steps(near, far, x_ref, o_ref, slots, part, slots_far, sn, rn, sf, rf):
    low, high, near_ids, far_ids = neighbours(near, far)
    copies = [
        send(x_ref, slots.at[low], sn.at[k], rn.at[k], target) for k, target in enumerate(near_ids)
    ]
    slots[low] = x_ref[...]
    yield
    for copy in copies:
        copy.wait()
    total = slots[0]
    for k in range(1, near):
        total = total + slots[k]
    part[...] = total
    copies = [
        send(part, slots_far.at[high], sf.at[k], rf.at[k], target)
        for k, target in enumerate(far_ids)
    ]
    slots_far[high] = total
    yield
    for copy in copies:
        copy.wait()
    total = slots_far[0]
    for k in range(1, far):
        total = total + slots_far[k]
    o_ref[...] = total
    yield


def greet_all(near, far):
    low, high, near_ids, far_ids = neighbours(near, far)
    greet(near_ids + far_ids)


def reduce_small_kernel(near, far, *refs):
    greet_all(near, far)
    for _ in small_steps(near, far, *refs):
        pass


def small_scratch(near, far, shape):
    return [
        pltpu.VMEM((near,) + shape, F32),
        pltpu.VMEM(shape, F32),
        pltpu.VMEM((far,) + shape, F32),
        pltpu.SemaphoreType.DMA((near,)),
        pltpu.SemaphoreType.DMA((near,)),
        pltpu.SemaphoreType.DMA((far,)),
        pltpu.SemaphoreType.DMA((far,)),
    ]


def reduce_small(x, size, collective_id):
    near = math.gcd(size, 4)
    far = size // near
    return pl.pallas_call(
        functools.partial(reduce_small_kernel, near, far),
        out_shape=jax.ShapeDtypeStruct(x.shape, F32),
        in_specs=[pl.BlockSpec(memory_space=pltpu.VMEM)],
        out_specs=pl.BlockSpec(memory_space=pltpu.VMEM),
        scratch_shapes=small_scratch(near, far, x.shape),
        compiler_params=pltpu.CompilerParams(collective_id=collective_id, has_side_effects=True),
    )(x)


def position():
    me = lax.axis_index("row")
    return me, lax.rem(me, 2), lax.rem(me // 2, 2), me // 4


def scatter_steps(parts, far, x_ref, half, quarter, landed, sems, small):
    me, core, side, high = position()
    peer_core = me + 1 - 2 * core
    peer_side = me + 2 - 4 * side
    far_ids = [lax.rem(high + k, far) for k in range(1, far)]
    sa, ra, sb, rb, sc, rc = sems
    first, second, third = [], [], []
    for k in range(parts):
        first.append(send(x_ref.at[k, :, :, 1 - core], half.at[k], sa.at[k], ra.at[k], peer_core))
    next(small)
    for k in range(parts):
        first[k].wait()
        half[k] = half[k] + x_ref[k, :, :, core]
        second.append(send(half.at[k, :, 1 - side], quarter.at[k], sb.at[k], rb.at[k], peer_side))
    next(small)
    for k in range(parts):
        second[k].wait()
        quarter[k] = quarter[k] + half[k, :, side]
        third.append(
            [
                send(
                    quarter.at[k, to],
                    landed.at[k, d],
                    sc.at[k, d],
                    rc.at[k, d],
                    to * 4 + lax.rem(me, 4),
                )
                for d, to in enumerate(far_ids)
            ]
        )
    next(small)
    for k in range(parts):
        total = quarter[k, high]
        for d, copy in enumerate(third[k]):
            copy.wait()
            total = total + landed[k, d]
        yield k, total


def gather_steps(parts, far, o_ref, values, sems, small):
    me, core, side, high = position()
    peer_core = me + 1 - 2 * core
    peer_side = me + 2 - 4 * side
    far_ids = [lax.rem(high + k, far) for k in range(1, far)]
    sa, ra, sb, rb, sc, rc = sems
    first, second, third = [], [], []
    for k, value in values:
        o_ref[k, high, side, core] = value
        mine = o_ref.at[k, high, side, core]
        first.append(
            [
                send(mine, mine, sa.at[k, d], ra.at[k, d], to * 4 + lax.rem(me, 4))
                for d, to in enumerate(far_ids)
            ]
        )
    next(small)
    for k in range(parts):
        for copy in first[k]:
            copy.wait()
        block = o_ref.at[k, :, side, core]
        second.append(send(block, block, sb.at[k], rb.at[k], peer_side))
    next(small)
    for k in range(parts):
        second[k].wait()
        block = o_ref.at[k, :, :, core]
        third.append(send(block, block, sc.at[k], rc.at[k], peer_core))
    next(small)
    for k in range(parts):
        third[k].wait()


def scatter_kernel(parts, far, x_ref, y_ref, o_ref, oy_ref, *refs):
    greet_all(4, far)
    small = small_steps(4, far, y_ref, oy_ref, *refs[9:])
    for k, total in scatter_steps(parts, far, x_ref, *refs[:3], refs[3:9], small):
        o_ref[k] = total


def gather_kernel(parts, far, x_ref, y_ref, o_ref, oy_ref, *refs):
    greet_all(4, far)
    small = small_steps(4, far, y_ref, oy_ref, *refs[6:])
    gather_steps(parts, far, o_ref, [(k, x_ref[k]) for k in range(parts)], refs[:6], small)


def reduce_phase(phase, far, x_ref, o_ref, half, quarter, landed, sems):
    me = lax.axis_index("row")
    core, side, high = lax.rem(me, 2), lax.rem(me // 2, 2), me // 4
    peer_core = me + 1 - 2 * core
    peer_side = me + 2 - 4 * side
    far_ids = [(d, lax.rem(high + d + 1, far)) for d in range(far - 1)]

    def copies(which):
        def make(src, dst, slot, target):
            return pltpu.make_async_remote_copy(
                src_ref=src,
                dst_ref=dst,
                send_sem=sems[2 * which].at[slot],
                recv_sem=sems[2 * which + 1].at[slot],
                device_id={"row": target},
                device_id_type=MESH,
            )

        if which == 0:
            return [make(x_ref.at[:, :, 1 - core], half, 0, peer_core)]
        if which == 1:
            return [make(half.at[:, 1 - side], quarter, 0, peer_side)]
        if which == 2:
            return [
                make(quarter.at[to], landed.at[d], d, to * 4 + lax.rem(me, 4)) for d, to in far_ids
            ]
        if which == 3:
            mine = o_ref.at[high, side, core]
            return [make(mine, mine, d, to * 4 + lax.rem(me, 4)) for d, to in far_ids]
        if which == 4:
            return [make(o_ref.at[:, side, core], o_ref.at[:, side, core], 0, peer_side)]
        return [make(o_ref.at[:, :, core], o_ref.at[:, :, core], 0, peer_core)]

    if phase > 0:
        for copy in copies(phase - 1):
            copy.wait()
    if phase == 1:
        half[...] = half[...] + x_ref[:, :, core]
    elif phase == 2:
        quarter[...] = quarter[...] + half[:, side]
    elif phase == 3:
        total = quarter[high]
        for d, _ in far_ids:
            total = total + landed[d]
        o_ref[high, side, core] = total
    if phase < 6:
        for copy in copies(phase):
            copy.start()


def scatter_scratch(parts, far, rows, lanes):
    return [
        pltpu.VMEM((parts, far, 2, rows, lanes), F32),
        pltpu.VMEM((parts, far, rows, lanes), F32),
        pltpu.VMEM((parts, far, rows, lanes), F32),
    ]


def dma(*shapes):
    return [pltpu.SemaphoreType.DMA(shape) for shape in shapes]


def scatter_sems(parts, far):
    return dma((parts,), (parts,), (parts,), (parts,), (parts, far), (parts, far))


def gather_sems(parts, far):
    return dma((parts, far), (parts, far), (parts,), (parts,), (parts,), (parts,))


def comm_call(kernel, x, y, out_shape, scratch, collective_id):
    return pl.pallas_call(
        kernel,
        out_shape=(jax.ShapeDtypeStruct(out_shape, F32), jax.ShapeDtypeStruct(y.shape, F32)),
        in_specs=[pl.BlockSpec(memory_space=pltpu.VMEM)] * 2,
        out_specs=(pl.BlockSpec(memory_space=pltpu.VMEM),) * 2,
        scratch_shapes=scratch,
        compiler_params=pltpu.CompilerParams(
            collective_id=collective_id, has_side_effects=True, vmem_limit_bytes=VMEM_LIMIT
        ),
    )(x, y)


def reduce_scatter(x, y, size, collective_id):
    parts, _, rows, lanes = x.shape
    far = size // 4
    return comm_call(
        functools.partial(scatter_kernel, parts, far),
        x.reshape(parts, far, 2, 2, rows, lanes),
        y,
        (parts, rows, lanes),
        scatter_scratch(parts, far, rows, lanes)
        + scatter_sems(parts, far)
        + small_scratch(4, far, y.shape),
        collective_id,
    )


def all_gather(x, y, size, collective_id):
    parts, rows, lanes = x.shape
    far = size // 4
    out, total = comm_call(
        functools.partial(gather_kernel, parts, far),
        x,
        y,
        (parts, far, 2, 2, rows, lanes),
        gather_sems(parts, far) + small_scratch(4, far, y.shape),
        collective_id,
    )
    return out.reshape(parts, size, rows, lanes), total


def contract(a, b, dim_a, dim_b):
    return lax.dot_general(a, b, (((dim_a,), (dim_b,)), ((), ())), preferred_element_type=F32)


def forward_kernel(width, chunks, x_ref, mask_ref, own_ref, mix_ref, bias_ref, row_ref, col_ref):
    stream_layers = mix_ref.shape[0]
    tall = mix_ref.shape[1]
    lane = lax.broadcasted_iota(jnp.int32, (width, tall), 1)
    sub = lax.broadcasted_iota(jnp.int32, (width, tall), 0)
    eye = (lax.rem(lane, width) == sub).astype(F32)
    sums = [[], []]
    for walker in range(2):
        spin_rows = mask_ref[walker]
        cols = [None] * (stream_layers + 1)
        for chunk in range(chunks):
            here = slice(chunk * tall, (chunk + 1) * tall)
            own = own_ref[walker, :, here]
            select = jnp.concatenate([eye * own[0:1], eye * own[1:2]], axis=0).astype(BF16)
            pair = x_ref[walker, here]
            for layer in range(stream_layers + 1):
                row_ref[walker, layer, :, here] = contract(spin_rows, pair, 1, 1)[:8]
                part = contract(select, pair, 1, 0)
                cols[layer] = part if chunk == 0 else cols[layer] + part
                if layer < stream_layers:
                    zvals = contract(mix_ref[layer], pair, 1, 0)
                    bend = jnp.tanh(zvals + bias_ref[layer])
                    pair = (bend + pair.astype(F32)).astype(BF16)
        sums[walker] = cols
    for layer in range(stream_layers + 1):
        both = jnp.concatenate([sums[0][layer], sums[1][layer]], axis=0)
        col_ref[layer, 0] = both.T


def pair_forward(pair, mask_rows, own_rows, mix, bias_tall, width):
    walkers, tall_all, electrons = pair.shape
    layers = mix.shape[0] + 1
    chunks = tall_all // mix.shape[1]
    return pl.pallas_call(
        functools.partial(forward_kernel, width, chunks),
        grid=(walkers // 2,),
        out_shape=(
            jax.ShapeDtypeStruct((walkers, layers, 8, tall_all), F32),
            jax.ShapeDtypeStruct((layers, walkers // 2, electrons, 4 * width), F32),
        ),
        in_specs=[
            pl.BlockSpec((2, tall_all, electrons), lambda w: (w, 0, 0)),
            pl.BlockSpec((2,) + mask_rows.shape[1:], lambda w: (w, 0, 0)),
            pl.BlockSpec((2, 8, tall_all), lambda w: (w, 0, 0)),
            pl.BlockSpec(mix.shape, lambda w: (0, 0, 0)),
            pl.BlockSpec(bias_tall.shape, lambda w: (0, 0, 0)),
        ],
        out_specs=(
            pl.BlockSpec((2, layers, 8, tall_all), lambda w: (w, 0, 0, 0)),
            pl.BlockSpec((layers, 1, electrons, 4 * width), lambda w: (0, w, 0, 0)),
        ),
        compiler_params=pltpu.CompilerParams(vmem_limit_bytes=VMEM_LIMIT),
    )(pair, mask_rows, own_rows, mix, bias_tall)


def backward_kernel(
    width,
    chunks,
    far,
    x_steps,
    spin_ref,
    x_ref,
    mask_ref,
    row_ref,
    col_ref,
    mix_ref,
    mix_back_ref,
    bias_ref,
    feat_ref,
    gw_ref,
    gb_ref,
    sum_ref,
    turned,
    half,
    quarter,
    landed,
    gathered,
    *sems,
):
    walker = pl.program_id(0)
    slots = x_steps * chunks
    starts = [slots * share // 32 for share in (0, 2, 9, 16, 23, 30)]

    tall = mix_ref.shape[1]
    electrons = x_ref.shape[2]
    each = tall // width
    parity = lax.rem(walker, 2)

    @pl.when(walker == 0)
    def _():
        gw_ref[...] = jnp.zeros_like(gw_ref)
        gb_ref[...] = jnp.zeros_like(gb_ref)

    @pl.when(parity == 0)
    def _():
        for level in range(2):
            turned[level] = col_ref[level, 0].T.reshape(4, width, electrons)

    def grad_mean(level, chunk):
        here = slice(chunk * tall, (chunk + 1) * tall)
        row = row_ref[0, :, here]
        high = row.astype(BF16).astype(F32)
        rest = row - high
        mid = rest.astype(BF16).astype(F32)
        low = rest - mid
        split = jnp.concatenate([high, mid, low, jnp.zeros_like(row)], axis=0).astype(BF16)
        rows = contract(split, mask_ref[0, level], 0, 0)
        cols = []
        for step in range(each):
            spin = spin_ref[walker, chunk * each + step]
            cols.append(turned[level, parity * 2 + 1 - spin])
        return rows + jnp.concatenate(cols, axis=0)

    for chunk in range(chunks):
        for phase, start in enumerate(starts):
            if start % chunks == chunk:

                @pl.when(walker == start // chunks)
                def _(phase=phase):
                    if phase == 0:
                        greet_all(4, far)
                    reduce_phase(phase, far, feat_ref, gathered, half, quarter, landed, sems)

        here = slice(chunk * tall, (chunk + 1) * tall)
        pair0 = x_ref[0, here]
        bend0 = jnp.tanh(contract(mix_ref[0], pair0, 1, 0) + bias_ref[0])
        pair1 = (bend0 + pair0.astype(F32)).astype(BF16)
        bend1 = jnp.tanh(contract(mix_ref[1], pair1, 1, 0) + bias_ref[1])
        grad2 = grad_mean(1, chunk)
        gz1 = (grad2 * (1.0 - bend1 * bend1)).astype(BF16)
        gw_ref[1] += contract(pair1, gz1, 1, 1)
        wide1 = gz1.astype(F32)
        gb_ref[1] += jnp.sum(wide1.reshape(each, width, electrons), axis=0)
        grad1 = grad2 + contract(mix_back_ref[1], gz1, 1, 0) + grad_mean(0, chunk)
        gz0 = (grad1 * (1.0 - bend0 * bend0)).astype(BF16)
        gw_ref[0] += contract(pair0, gz0, 1, 1)
        gb_ref[0] += jnp.sum(gz0.astype(F32).reshape(each, width, electrons), axis=0)

    @pl.when(walker == pl.num_programs(0) - 1)
    def _():
        reduce_phase(6, far, feat_ref, gathered, half, quarter, landed, sems)
        sum_ref[...] = gathered[...]


def pair_backward(
    own_spins,
    pair,
    mask_pairs,
    row_parts,
    col_all,
    mix,
    mix_back,
    bias_tall,
    feats,
    width,
    size,
    collective_id,
):
    far = size // 4
    total, lanes = feats.shape
    padded = -(-total // (8 * size)) * 8 * size
    rows = padded // size
    shape = (far, 2, 2, rows, lanes)
    feats = jnp.pad(feats, ((0, padded - total), (0, 0))).reshape(shape)
    walkers, tall_all, electrons = pair.shape
    tall = mix.shape[1]
    gw, gb, sums = pl.pallas_call(
        functools.partial(backward_kernel, width, tall_all // tall, far, walkers),
        grid=(walkers,),
        out_shape=(
            jax.ShapeDtypeStruct((2, tall, tall), F32),
            jax.ShapeDtypeStruct((2, width, electrons), F32),
            jax.ShapeDtypeStruct(shape, F32),
        ),
        in_specs=[
            pl.BlockSpec(memory_space=pltpu.SMEM),
            pl.BlockSpec((1, tall_all, electrons), lambda w: (w, 0, 0)),
            pl.BlockSpec((1,) + mask_pairs.shape[1:], lambda w: (w, 0, 0, 0)),
            pl.BlockSpec((1, 8, tall_all), lambda w: (w, 0, 0)),
            pl.BlockSpec((2, 1, electrons, 4 * width), lambda w: (0, w // 2, 0, 0)),
            pl.BlockSpec(mix.shape, lambda w: (0, 0, 0)),
            pl.BlockSpec(mix.shape, lambda w: (0, 0, 0)),
            pl.BlockSpec(bias_tall.shape, lambda w: (0, 0, 0)),
            pl.BlockSpec(memory_space=pltpu.VMEM),
        ],
        out_specs=(
            pl.BlockSpec((2, tall, tall), lambda w: (0, 0, 0)),
            pl.BlockSpec((2, width, electrons), lambda w: (0, 0, 0)),
            pl.BlockSpec(memory_space=pltpu.VMEM),
        ),
        scratch_shapes=[
            pltpu.VMEM((2, 4, width, electrons), F32),
            pltpu.VMEM((far, 2, rows, lanes), F32),
            pltpu.VMEM((far, rows, lanes), F32),
            pltpu.VMEM((far, rows, lanes), F32),
            pltpu.VMEM(shape, F32),
        ]
        + dma((1,), (1,), (1,), (1,), (far,), (far,), (far,), (far,), (1,), (1,), (1,), (1,)),
        compiler_params=pltpu.CompilerParams(
            vmem_limit_bytes=VMEM_LIMIT, collective_id=collective_id, has_side_effects=True
        ),
    )(own_spins, pair, mask_pairs, row_parts, col_all, mix, mix_back, bias_tall, feats)
    return gw, gb, sums.reshape(padded, lanes)


def general(
    size,
    one_input,
    pair_input,
    spins,
    cotangent,
    w_self,
    w_means,
    w_rows,
    w_cols,
    b_one,
    w_pair,
    b_pair,
):
    highest = lax.Precision.HIGHEST
    walkers, rows_dev, one_width = one_input.shape
    width = pair_input.shape[2]
    electrons = pair_input.shape[3]
    layers = w_self.shape[0]
    flat = walkers * rows_dev
    tall_all = rows_dev * width
    each = math.gcd(rows_dev, 8)
    tall = each * width
    row_start = lax.axis_index("row") * rows_dev

    up_mask = (spins == 1).astype(F32)
    masks = jnp.stack([up_mask, 1.0 - up_mask], axis=1)
    counts = jnp.sum(masks, axis=2)
    own_spins = lax.dynamic_slice_in_dim((spins == 1).astype(jnp.int32), row_start, rows_dev, 1)
    own_mask = lax.dynamic_slice_in_dim(masks, row_start, rows_dev, 2)
    own_up = own_mask[:, 0, :, None] > 0.5

    eye = jnp.eye(each, dtype=BF16)
    mix = jnp.stack([jnp.kron(eye, w_pair[k].T) for k in range(layers - 1)])
    mix_back = jnp.stack([jnp.kron(eye, w_pair[k]) for k in range(layers - 1)])
    bias_tall = jnp.tile(b_pair, (1, each))[:, :, None]
    mask_rows = jnp.pad(masks, ((0, 0), (0, 14), (0, 0))).astype(BF16)
    own_rows = jnp.pad(jnp.repeat(own_mask, width, axis=2), ((0, 0), (0, 6), (0, 0)))
    pair_flat = pair_input.reshape(walkers, tall_all, electrons)

    row_sums, col_part = pair_forward(pair_flat, mask_rows, own_rows, mix, bias_tall, width)
    sum_parts = 2 * layers
    col_part = col_part.reshape(sum_parts, walkers // 4, size, rows_dev, 4 * width)
    col_part = jnp.transpose(col_part, (0, 2, 1, 3, 4)).reshape(sum_parts, size, -1, 4 * width)
    walker_eye = jnp.eye(walkers, dtype=F32)
    gather_mask = (walker_eye[:, None, :, None] * own_mask[:, :, None, :]).reshape(
        2 * walkers, flat
    )
    gather_mask = gather_mask.astype(BF16)
    one_cur = one_input.reshape(flat, one_width)
    first_part = jnp.dot(gather_mask, one_cur, preferred_element_type=F32)
    col_sums, first_sums = reduce_scatter(col_part, first_part, size, 0)
    col_sums = col_sums.reshape(layers, walkers // 2, rows_dev, 2, 2 * width)
    col_sums = jnp.transpose(col_sums, (0, 1, 3, 2, 4)).reshape(
        layers, walkers, rows_dev, 2, width
    )
    row_sums = jnp.transpose(
        row_sums[:, :, :2].reshape(walkers, layers, 2, rows_dev, width), (1, 0, 3, 2, 4)
    )
    scale = counts[None, :, None, :, None]
    row_means = (row_sums / scale).astype(BF16).reshape(layers, flat, 2 * width)
    col_means = (col_sums / scale).astype(BF16).reshape(layers, flat, 2 * width)

    w_all = jnp.concatenate([w_self, w_rows, w_cols], axis=1)
    counts_flat = counts.reshape(2 * walkers, 1)

    stored = []
    for layer in range(layers):
        if layer == 0:
            one_sums = first_sums
        else:
            part_one = jnp.dot(gather_mask, one_cur, preferred_element_type=F32)
            one_sums = reduce_small(part_one, size, 1 + layer)
        one_means = (one_sums / counts_flat).astype(BF16).reshape(walkers, 2 * one_width)
        feats = jnp.concatenate([one_cur, row_means[layer], col_means[layer]], axis=1)
        shared = jnp.dot(one_means, w_means[layer], preferred_element_type=F32) + b_one[layer]
        preact = jnp.dot(feats, w_all[layer], preferred_element_type=F32)
        preact = preact.reshape(walkers, rows_dev, one_width) + shared[:, None, :]
        activation = jnp.tanh(preact)
        stored.append((feats, one_means, activation))
        one_cur = (activation + one_cur.reshape(preact.shape).astype(F32)).astype(BF16)
        one_cur = one_cur.reshape(flat, one_width)
    one_output = one_cur.reshape(walkers, rows_dev, one_width)

    grad_one = cotangent
    feat_grads = [None] * layers
    pre_totals = [None] * layers
    row_parts = []
    col_parts = []
    for layer in reversed(range(layers)):
        feats, one_means, activation = stored[layer]
        grad_pre = (grad_one * (1.0 - activation * activation)).astype(BF16)
        pre_sums = jnp.sum(grad_pre.astype(F32), axis=1)
        flat_pre = grad_pre.reshape(flat, one_width)
        feat_grads[layer] = lax.dot_general(
            feats, flat_pre, (((0,), (0,)), ((), ())), preferred_element_type=F32
        )
        if layer == 0:
            pre_totals[0] = pre_sums
            break
        grad_feat = lax.dot_general(
            flat_pre, w_all[layer], (((1,), (1,)), ((), ())), preferred_element_type=F32
        ).reshape(walkers, rows_dev, one_width + 4 * width)
        side_scale = counts[:, None, :, None]
        row_grad = grad_feat[:, :, one_width : one_width + 2 * width]
        row_grad = row_grad.reshape(walkers, rows_dev, 2, width) / side_scale
        row_parts.append(jnp.transpose(row_grad, (0, 2, 1, 3)).reshape(walkers, 2, tall_all))
        col_grad = grad_feat[:, :, one_width + 2 * width :]
        col_grad = (col_grad.reshape(walkers, rows_dev, 2, width) / side_scale).reshape(
            walkers // 2, 2, rows_dev, 2 * width
        )
        col_parts.append(jnp.transpose(col_grad, (0, 2, 1, 3)).reshape(-1, 4 * width))
        if layer == 1:
            col_all, pre_totals[layer] = all_gather(
                jnp.concatenate([col_parts[1], col_parts[0]]).reshape(4, -1, 4 * width),
                pre_sums,
                size,
                2 + 2 * layers,
            )
        else:
            pre_totals[layer] = reduce_small(pre_sums, size, 1 + layers + layer)
        mean_total = jnp.einsum(
            "wh,ah->wa", pre_totals[layer], w_means[layer].astype(F32), precision=highest
        )
        mean_total = mean_total.reshape(walkers, 2, one_width) / counts[:, :, None]
        grad_one = (
            grad_one
            + grad_feat[:, :, :one_width]
            + jnp.where(own_up, mean_total[:, None, 0], mean_total[:, None, 1])
        )

    row_stack = jnp.concatenate(
        [row_parts[1], row_parts[0], jnp.zeros((walkers, 4, tall_all), F32)], axis=1
    )
    col_all = col_all.reshape(4, size, walkers // 4, rows_dev, 4 * width)
    col_all = jnp.transpose(col_all, (0, 2, 1, 3, 4)).reshape(
        2, walkers // 2, electrons, 4 * width
    )
    lower = jnp.pad(masks, ((0, 0), (0, 6), (0, 0)))
    upper = jnp.pad(masks, ((0, 0), (2, 4), (0, 0)))
    mask_pairs = jnp.stack(
        [
            jnp.concatenate([piece, piece, piece, jnp.zeros_like(piece)], axis=1)
            for piece in (lower, upper)
        ],
        axis=1,
    ).astype(BF16)
    gw, gb, feat_sums = pair_backward(
        own_spins,
        pair_flat,
        mask_pairs,
        row_stack,
        col_all,
        mix,
        mix_back,
        bias_tall,
        jnp.concatenate(feat_grads, axis=0),
        width,
        size,
        3 + 2 * layers,
    )
    g_wpair = jnp.einsum("lacad->lcd", gw.reshape(layers - 1, each, width, each, width))
    g_bpair = jnp.sum(gb, axis=2)

    tail = jnp.concatenate([g_wpair.reshape(-1), g_bpair.reshape(-1)])
    unit = 8 * one_width
    tail = jnp.pad(tail, (0, -tail.size % unit)).reshape(-1, one_width)
    ends = reduce_small(jnp.concatenate([pre_totals[0], tail], axis=0), size, 4 + 2 * layers)
    deep = one_width + 4 * width
    first = feat_sums[: layers * deep].reshape(layers, deep, one_width)
    pre_totals[0] = ends[:walkers]
    tail = ends[walkers:].reshape(-1)
    square = width * width
    pre_all = jnp.stack(pre_totals)
    means_all = jnp.stack([item[1] for item in stored]).astype(F32)
    grad_means = jnp.einsum("lwa,lwk->lak", means_all, pre_all, precision=highest)
    count = layers - 1
    return (
        one_output,
        first[:, :one_width],
        grad_means,
        first[:, one_width : one_width + 2 * width],
        first[:, one_width + 2 * width :],
        jnp.sum(pre_all, axis=1),
        tail[: count * square].reshape(count, width, width),
        tail[count * square : count * square + count * width].reshape(count, width),
    )


def iota(shape, dim):
    return lax.broadcasted_iota(jnp.int32, shape, dim)


def split3(x):
    high = x.astype(BF16).astype(F32)
    rest = x - high
    mid = rest.astype(BF16).astype(F32)
    return jnp.concatenate([high, mid, rest - mid], axis=0).astype(BF16)


class Place:
    def __init__(self, far):
        self.far = far
        self.me, self.core, self.side, self.high = position()
        self.low = lax.rem(self.me, 4)
        self.peer_core = self.me + 1 - 2 * self.core
        self.peer_side = self.me + 2 - 4 * self.side
        self.far_ids = [
            (d, lax.rem(self.high + d + 1, far), lax.rem(self.high + d + 1, far) * 4 + self.low)
            for d in range(far - 1)
        ]
        self.near_ids = [(d, self.high * 4 + lax.rem(self.low + d + 1, 4)) for d in range(3)]


def remote(src, dst, send_sem, recv_sem, target):
    return pltpu.make_async_remote_copy(
        src_ref=src,
        dst_ref=dst,
        send_sem=send_sem,
        recv_sem=recv_sem,
        device_id={"row": target},
        device_id_type=MESH,
    )


class SmallSum:
    def __init__(self, place, across, within, sems):
        self.place, self.across, self.within = place, across, within
        self.sems = sems

    def far_copies(self, k):
        sf, rf, _, _ = self.sems
        mine = self.across.at[k, self.place.high]
        return [
            remote(mine, mine, sf.at[k, d], rf.at[k, d], target)
            for d, _, target in self.place.far_ids
        ]

    def near_copies(self, k):
        _, _, sn, rn = self.sems
        mine = self.within.at[k, self.place.low]
        return [
            remote(mine, mine, sn.at[k, d], rn.at[k, d], target)
            for d, target in self.place.near_ids
        ]

    def start(self, k, value):
        self.across[k, self.place.high] = value
        for copy in self.far_copies(k):
            copy.start()

    def middle(self, k):
        for copy in self.far_copies(k):
            copy.wait()
        total = self.across[k, 0]
        for n in range(1, self.place.far):
            total = total + self.across[k, n]
        self.within[k, self.place.low] = total
        for copy in self.near_copies(k):
            copy.start()

    def finish(self, k):
        for copy in self.near_copies(k):
            copy.wait()
        total = self.within[k, 0]
        for n in range(1, 4):
            total = total + self.within[k, n]
        return total


class ColumnSums:
    def __init__(self, place, source, half, quarter, landed, total, sems):
        self.place, self.source, self.half, self.quarter = place, source, half, quarter
        self.landed, self.total, self.sems = landed, total, sems

    def first(self, k):
        sa, ra = self.sems[0:2]
        p = self.place
        return remote(
            self.source.at[k, :, :, 1 - p.core], self.half.at[k], sa.at[k], ra.at[k], p.peer_core
        )

    def second(self, k):
        sb, rb = self.sems[2:4]
        p = self.place
        return remote(
            self.half.at[k, :, 1 - p.side], self.quarter.at[k], sb.at[k], rb.at[k], p.peer_side
        )

    def third(self, k):
        sc, rc = self.sems[4:6]
        return [
            remote(
                self.quarter.at[k, z], self.landed.at[k, d], sc.at[k, d], rc.at[k, d], target
            )
            for d, z, target in self.place.far_ids
        ]

    def a(self, k):
        self.first(k).start()

    def b(self, k):
        self.first(k).wait()
        self.half[k] = self.half[k] + self.source[k, :, :, self.place.core]
        self.second(k).start()

    def c(self, k):
        self.second(k).wait()
        self.quarter[k] = self.quarter[k] + self.half[k, :, self.place.side]
        for copy in self.third(k):
            copy.start()

    def d(self, k):
        for copy in self.third(k):
            copy.wait()
        total = self.quarter[k, self.place.high]
        for n in range(self.place.far - 1):
            total = total + self.landed[k, n]
        self.total[k] = total


class Gather:
    def __init__(self, place, ref, sems):
        self.place, self.ref, self.sems = place, ref, sems

    def far_copies(self, k):
        p = self.place
        sa, ra = self.sems[0:2]
        mine = self.ref.at[k, p.high, p.side, p.core]
        return [remote(mine, mine, sa.at[k, d], ra.at[k, d], target) for d, _, target in p.far_ids]

    def side_copies(self, k):
        p = self.place
        sb, rb = self.sems[2:4]
        got = []
        for d in range(p.far):
            block = self.ref.at[k, lax.rem(p.high - d - 1 + p.far, p.far), p.side, p.core]
            got.append(remote(block, block, sb.at[k, d], rb.at[k, d], p.peer_side))
        return got

    def core_copy(self, k):
        p = self.place
        sc, rc = self.sems[4:6]
        block = self.ref.at[k, :, :, p.core]
        return remote(block, block, sc.at[k], rc.at[k], p.peer_core)

    def step(self, k, phase):
        if phase == 0:
            for copy in self.far_copies(k):
                copy.start()
            self.side_copies(k)[-1].start()
        elif phase == 1:
            onward = self.side_copies(k)
            for d, copy in enumerate(self.far_copies(k)):
                copy.wait()
                onward[d].start()
        elif phase == 2:
            for copy in self.side_copies(k):
                copy.wait()
            self.core_copy(k).start()
        else:
            self.core_copy(k).wait()


def whole_kernel(
    dims,
    one_ref,
    pair_hbm,
    spins_ref,
    cot_ref,
    wself_ref,
    wmeans_ref,
    wrows_ref,
    wcols_ref,
    bone_ref,
    wpair_ref,
    bpair_ref,
    oneout_ref,
    feat_all,
    means,
    pre_all,
    gtail_ref,
    pair0,
    pair1,
    slope0,
    slope1,
    mask16,
    sel,
    mix,
    mix_back,
    bias,
    wbig,
    gmask,
    upcol,
    coef,
    cg,
    cnt_y,
    ysum,
    feats,
    act,
    grad_one,
    col_two,
    rhs,
    gw,
    cs_source,
    cs_half,
    cs_quarter,
    cs_landed,
    cs_total,
    ag_ref,
    fs_across,
    fs_within,
    bs_across,
    bs_within,
    es_across,
    es_within,
    feat_ref,
    feat_half,
    feat_quarter,
    feat_landed,
    load_sem,
    again_sem,
    *sems,
):
    walkers, rows, width, electrons, one_width, layers, far, tall = dims
    flat = walkers * rows
    tall_all = rows * width
    chunks = tall_all // tall
    each = tall // width
    pairs = walkers // 2
    place = Place(far)

    loads = [
        pltpu.make_async_copy(pair_hbm.at[w], pair0.at[w], load_sem.at[w]) for w in range(walkers)
    ]
    for load in loads:
        load.start()
    again = [
        pltpu.make_async_copy(pair_hbm.at[w], pair0.at[w], again_sem.at[w]) for w in range(walkers)
    ]

    barrier = pltpu.get_barrier_semaphore()
    peers = [t for _, _, t in place.far_ids] + [t for _, t in place.near_ids]
    for target in peers:
        pl.semaphore_signal(barrier, inc=1, device_id={"row": target}, device_id_type=MESH)

    sems = list(sems)

    def take(n):
        got = sems[:n]
        del sems[:n]
        return got

    columns = ColumnSums(place, cs_source, cs_half, cs_quarter, cs_landed, cs_total, take(6))
    gather = Gather(place, ag_ref, take(6))
    fwd_sum = SmallSum(place, fs_across, fs_within, take(4))
    bwd_sum = SmallSum(place, bs_across, bs_within, take(4))
    end_sum = SmallSum(place, es_across, es_within, take(4))
    feat_sems = take(12)

    up = (spins_ref[...] == 1).astype(F32)
    down = 1.0 - up
    count_up = jnp.sum(up, axis=1, keepdims=True)
    count_down = jnp.sum(down, axis=1, keepdims=True)
    counts16 = jnp.concatenate([count_up, count_down], axis=0)
    both_spins = jnp.concatenate([up, down], axis=0).astype(BF16)
    first_row = place.me * rows

    pick = (iota((electrons, flat), 0) == first_row + lax.rem(iota((electrons, flat), 1), rows))
    own = contract(both_spins, pick.astype(BF16), 1, 0)
    same = lax.rem(iota((2 * walkers, flat), 0), walkers) == iota((2 * walkers, flat), 1) // rows
    gmask[...] = jnp.where(same, own, 0.0).astype(BF16)
    fwd_partial = contract(gmask[...], one_ref[...], 1, 0)
    pl.semaphore_wait(barrier, len(peers))
    fwd_sum.start(0, fwd_partial)

    lane = iota((width, tall), 1)
    eye_tall = (lax.rem(iota((tall, width), 0), width) == iota((tall, width), 1)).astype(BF16)
    same_block = iota((tall, tall), 0) // width == iota((tall, tall), 1) // width
    for k in range(layers - 1):
        for target, dim in ((mix, 1), (mix_back, 0)):
            part = contract(eye_tall, wpair_ref[k], 1, dim).astype(BF16)
            full = contract(part, eye_tall, 1, 1)
            target[k] = jnp.where(same_block, full, 0.0).astype(BF16)
        bias[k] = jnp.sum(eye_tall.astype(F32) * bpair_ref[k : k + 1, :], axis=1, keepdims=True)

    spread = iota((electrons, tall_all), 0) == first_row + iota((electrons, tall_all), 1) // width
    own_rows = contract(both_spins, spread.astype(BF16), 1, 0)
    eye_wide = (lax.rem(iota((width, tall_all), 1), width) == iota((width, tall_all), 0)).astype(F32)
    row_id = iota((16, electrons), 0)
    for w in range(walkers):
        mask16[w] = jnp.where(
            row_id == 0, up[w : w + 1], jnp.where(row_id == 1, down[w : w + 1], 0.0)
        ).astype(BF16)
        sel[w] = jnp.concatenate(
            [eye_wide * own_rows[w : w + 1], eye_wide * own_rows[walkers + w : walkers + w + 1]],
            axis=0,
        ).astype(BF16)

    def walker_counts(w, lanes, period):
        is_up = lax.rem(iota((1, lanes), 1), 2 * period) < period
        return jnp.where(is_up, count_up[w : w + 1], count_down[w : w + 1])

    for w in range(walkers):
        cg[w] = jnp.broadcast_to(walker_counts(w, 4 * width, width), (rows, 4 * width))
        cnt_y[w] = jnp.broadcast_to(walker_counts(w, 8 * width, 4 * width), (8, 8 * width))
    which = lax.rem(iota((2 * walkers, 4 * width), 1), 2 * width) // width
    chooser = (iota((2 * walkers, 4 * width), 0) // walkers == which).astype(BF16)
    own_cols = contract(gmask[...], chooser, 0, 0)
    for level in range(2):
        coef[level, :, 4 * width :] = own_cols
    is_up_row = (iota((2 * walkers, one_width), 0) < walkers).astype(BF16)
    upcol[...] = contract(gmask[...], is_up_row, 0, 0)
    for k in range(layers):
        wbig[k, :one_width] = wself_ref[k]
        for start, ref in ((0, wrows_ref), (4, wcols_ref)):
            for copy in range(2):
                low = one_width + (start + 2 * copy) * width
                wbig[k, low : low + 2 * width] = ref[k]

    def row_sums(layer, w, chunk, pair):
        got = contract(mask16[w], pair, 1, 1)
        for k in range(tall // 128):
            for s in range(2):
                ysum[layer, w, pl.ds(chunk * (tall // 128) + k, 1), s * 128 : (s + 1) * 128] = got[
                    s : s + 1, k * 128 : (k + 1) * 128
                ]

    def stream(layer, w, slot, source, source_w, slopes, target, target_w):
        cols = None
        for chunk in range(chunks):
            here = slice(chunk * tall, (chunk + 1) * tall)
            pair = source[source_w, here]
            row_sums(layer, w, chunk, pair)
            left = jnp.concatenate([mix[layer], sel[w, :, here]], axis=0)
            both = contract(left, pair, 1, 0)
            part = both[tall:]
            cols = part if cols is None else cols + part
            bend = jnp.tanh(both[:tall] + bias[layer])
            slopes[w, here] = (1.0 - bend * bend).astype(BF16)
            target[target_w, here] = (bend + pair.astype(F32)).astype(BF16)
        col_two[slot] = cols

    def sums_only(layer, w, slot):
        cols = None
        for chunk in range(chunks):
            here = slice(chunk * tall, (chunk + 1) * tall)
            pair = pair0[w, here]
            row_sums(layer, w, chunk, pair)
            part = contract(sel[w, :, here], pair, 1, 0)
            cols = part if cols is None else cols + part
        col_two[slot] = cols

    lags = ((1, columns.b), (4, columns.c), (7, columns.d))

    def tick(t):
        both = col_two[...].reshape(4 * width, electrons)
        cs_source[t] = both.T.reshape(far, 2, 2, rows, 4 * width)
        columns.a(t)
        for lag, step in lags:

            @pl.when(t >= lag)
            def _(lag=lag, step=step):
                step(t - lag)

    def part_of(layer, p):
        return layer * pairs + p

    def one_layer(layer):
        totals = fwd_sum.finish(layer)
        mean = (totals / counts16).astype(BF16)
        means[layer] = mean
        ups = contract(mean, wmeans_ref[layer, :one_width], 1, 0)
        downs = contract(mean, wmeans_ref[layer, one_width:], 1, 0)
        shared = ups[:walkers] + downs[walkers:] + bone_ref[layer : layer + 1, :]
        lanes = 8 * width
        ys = (ysum[layer] / cnt_y[...]).reshape(walkers * 8, lanes).astype(BF16)
        per = rows // 8
        expand = iota((flat, walkers * 8), 0) // per == iota((flat, walkers * 8), 1)
        wide = contract(expand.astype(BF16), ys, 1, 0)
        keep = lax.rem(iota((flat, lanes), 1) // width, 4) == lax.rem(iota((flat, lanes), 0), per)
        wide = jnp.where(keep, wide, 0.0).astype(BF16)
        src, dst = iota((lanes, 4 * width), 0), iota((lanes, 4 * width), 1)
        fold = (src // (4 * width)) * width + lax.rem(src, width) == dst
        row_mean = contract(wide, fold.astype(BF16), 1, 0)
        first_half = iota((rows, 4 * width), 1) < 2 * width
        col_mean = []
        for p in range(pairs):
            total = cs_total[part_of(layer, p)]
            col_mean.append(jnp.where(first_half, total / cg[2 * p], 0.0))
            col_mean.append(jnp.where(first_half, 0.0, total / cg[2 * p + 1]))
        current = one_ref[...] if layer == 0 else oneout_ref[...]
        feats[layer, :, :one_width] = current
        feats[layer, :, one_width : one_width + 4 * width] = row_mean.astype(BF16)
        feats[layer, :, one_width + 4 * width :] = jnp.concatenate(col_mean, axis=0).astype(BF16)
        preact = contract(feats[layer], wbig[layer], 1, 0)
        for w in range(walkers):
            here = slice(w * rows, (w + 1) * rows)
            bend = jnp.tanh(preact[here] + shared[w : w + 1])
            act[layer, here] = bend
            oneout_ref[here] = (bend + current[here].astype(F32)).astype(BF16)
        if layer + 1 < layers:
            fwd_sum.start(layer + 1, contract(gmask[...], oneout_ref[...], 1, 0))

    def load_wait(w):
        for k in range(walkers):

            @pl.when(w == k)
            def _(k=k):
                loads[k].wait()

    def pass0(p, carry):
        def body(slot, inner):
            w = 2 * p + slot
            load_wait(w)
            stream(0, w, slot, pair0, w, slope0, pair1, w)
            return inner

        lax.fori_loop(0, 2, body, 0)
        tick(p)

        @pl.when(p == 1)
        def _():
            fwd_sum.middle(0)

        return carry

    lax.fori_loop(0, pairs, pass0, 0)

    def pass1(p, carry):
        def body(slot, inner):
            w = 2 * p + slot
            stream(1, w, slot, pair1, w, slope1, pair0, w)
            return inner

        lax.fori_loop(0, 2, body, 0)
        tick(pairs + p)
        return carry

    lax.fori_loop(0, pairs, pass1, 0)

    def pass2(p, carry):
        def body(slot, inner):
            sums_only(2, 2 * p + slot, slot)
            return inner

        lax.fori_loop(0, 2, body, 0)
        tick(2 * pairs + p)

        @pl.when(p == 2)
        def _():
            one_layer(0)

        return carry

    lax.fori_loop(0, pairs, pass2, 0)
    for load in again:
        load.start()
    columns.b(11)
    columns.c(8)
    columns.d(5)
    columns.c(9)
    fwd_sum.middle(1)
    columns.d(6)
    columns.c(10)
    columns.d(7)
    columns.c(11)
    one_layer(1)
    columns.d(8)
    columns.d(9)
    fwd_sum.middle(2)
    columns.d(10)
    columns.d(11)
    one_layer(2)

    walker_sum = (iota((16, flat), 0) == iota((16, flat), 1) // rows).astype(BF16)
    blocks = 4 * far
    deep = one_width + 4 * width
    block_rows = deep // blocks

    def cotangents(layer, level):
        grad = cot_ref[...] if layer == layers - 1 else grad_one[...]
        bend = act[layer]
        pre = (grad * (1.0 - bend * bend)).astype(BF16)
        index = layers - 1 - layer
        bwd_sum.start(index, contract(walker_sum, pre, 1, 0)[:walkers])
        if layer > 0:
            back = contract(pre, wbig[layer], 1, 1)
            grad_one[...] = grad + back[:, :one_width]
            counts = cg[...].reshape(flat, 4 * width)
            col = back[:, one_width + 4 * width :] / counts
            first_half = iota((rows, 4 * width), 1) < 2 * width
            for p in range(pairs):
                even = col[2 * p * rows : (2 * p + 1) * rows]
                odd = col[(2 * p + 1) * rows : (2 * p + 2) * rows]
                ag_ref[level, place.high, place.side, place.core, p] = jnp.where(
                    first_half, even, odd
                )
            gather.step(level, 0)
            row = back[:, one_width : one_width + 4 * width] / counts
            if layer < layers - 1:
                row = row + coef[1 - level, :, : 4 * width]
            coef[level, :, : 4 * width] = row
        grads = contract(feats[layer], pre, 0, 0)
        cols_at = one_width + 4 * width
        kept = jnp.concatenate(
            [
                grads[: one_width + 2 * width],
                grads[cols_at : cols_at + 2 * width] + grads[cols_at + 2 * width :],
            ],
            axis=0,
        )
        for b in range(blocks):
            feat_ref[layer, b // 4, (b // 2) % 2, b % 2] = kept[b * block_rows : (b + 1) * block_rows]

    def finish_pre(layer):
        total = bwd_sum.finish(layers - 1 - layer)
        pre_all[layer] = total
        return split3(total)

    def feat(layer, phase):
        reduce_phase(
            phase,
            far,
            feat_ref.at[layer],
            feat_all.at[layer],
            feat_half.at[layer],
            feat_quarter.at[layer],
            feat_landed.at[layer],
            [sem.at[layer] for sem in feat_sems],
        )

    def spread_means(layer):
        pieces = finish_pre(layer)
        back = contract(pieces, wmeans_ref[layer], 1, 1)
        total = back[:walkers] + back[walkers : 2 * walkers] + back[2 * walkers :]
        mean_up = total[:, :one_width] / count_up
        mean_down = total[:, one_width:] / count_down
        for w in range(walkers):
            here = slice(w * rows, (w + 1) * rows)
            grad_one[here] = grad_one[here] + jnp.where(
                upcol[here] > 0.5, mean_up[w : w + 1], mean_down[w : w + 1]
            )

    cotangents(2, 0)
    feat(2, 0)
    bwd_sum.middle(0)
    gather.step(0, 1)
    spread_means(2)
    cotangents(1, 1)
    feat(1, 0)
    bwd_sum.middle(1)
    gather.step(0, 2)
    feat(2, 1)
    spread_means(1)
    cotangents(0, 0)
    feat(0, 0)
    feat(1, 1)
    feat(2, 2)
    for load in again:
        load.wait()

    first_half = iota((flat, 4 * width), 1) < 2 * width
    for level in range(2):
        row = coef[level, :, : 4 * width]
        lead = row.astype(BF16).astype(F32)
        coef[level, :, : 4 * width] = jnp.where(first_half, lead, row - lead)

    gw[...] = jnp.zeros_like(gw)
    gather.step(0, 3)

    lane_eye = (
        lax.rem(iota((width, 8 * width), 1), width) == iota((width, 8 * width), 0)
    ).astype(F32)
    ones = jnp.ones((16, electrons), BF16)
    spin_of = lax.rem(iota((4 * width, electrons), 0), 2 * width) < width

    def prepare(level, p):
        turned = []
        for n in range(level + 1):
            block = ag_ref[n, :, :, :, p].reshape(electrons, 4 * width)
            turned.append(block)
        total = turned[0] if level == 0 else turned[0] + turned[1]
        total = total.T
        for slot in range(2):
            mine = total[slot * 2 * width : (slot + 1) * 2 * width]
            lead = mine.astype(BF16)
            rhs[slot, 4 * width : 6 * width] = lead
            rhs[slot, 6 * width :] = (mine - lead.astype(F32)).astype(BF16)
            spins = mask16[2 * p + slot].astype(F32)
            rhs[slot, : 4 * width] = jnp.where(spin_of, spins[0:1], spins[1:2]).astype(BF16)

    def spread_coef(level, w, chunk):
        pieces = []
        for e in range(each):
            line = coef[level, pl.ds(w * rows + chunk * each + e, 1), :]
            pieces.append(lane_eye * line)
        return jnp.concatenate(pieces, axis=0).astype(BF16)

    def level_one(p, slot):
        w = 2 * p + slot
        for chunk in range(chunks):
            here = slice(chunk * tall, (chunk + 1) * tall)
            grad = contract(spread_coef(0, w, chunk), rhs[slot], 1, 0)
            gz = (grad * slope1[w, here].astype(F32)).astype(BF16)
            slope1[w, here] = gz
            gw[1] += contract(jnp.concatenate([pair1[w, here], ones], axis=0), gz, 1, 1)

    def level_zero(p, slot):
        w = 2 * p + slot
        for chunk in range(chunks):
            here = slice(chunk * tall, (chunk + 1) * tall)
            left = jnp.concatenate([mix_back[1], spread_coef(1, w, chunk)], axis=1)
            right = jnp.concatenate([slope1[w, here], rhs[slot]], axis=0)
            grad = contract(left, right, 1, 0)
            gz = (grad * slope0[w, here].astype(F32)).astype(BF16)
            gw[0] += contract(jnp.concatenate([pair0[w, here], ones], axis=0), gz, 1, 1)

    def run(level, work, after):
        def step(p, carry):
            prepare(level, p)

            def body(slot, inner):
                work(p, slot)
                for at, todo in after:

                    @pl.when(2 * p + slot == at)
                    def _(todo=todo):
                        todo()

                return inner

            lax.fori_loop(0, 2, body, 0)
            return carry

        lax.fori_loop(0, pairs, step, 0)

    def at(step, work, *args):
        return step, lambda: work(*args)

    run(
        0,
        level_one,
        [
            at(0, feat, 0, 1),
            at(1, gather.step, 1, 1),
            at(1, bwd_sum.middle, 2),
            at(2, feat, 2, 3),
            at(3, feat, 1, 2),
            at(4, gather.step, 1, 2),
            at(5, feat, 0, 2),
            at(5, finish_pre, 0),
            at(6, feat, 2, 4),
            at(7, feat, 1, 3),
        ],
    )
    gather.step(1, 3)
    run(
        1,
        level_zero,
        [
            at(0, feat, 0, 3),
            at(1, feat, 2, 5),
            at(2, feat, 1, 4),
            at(3, feat, 0, 4),
            at(4, feat, 2, 6),
            at(5, feat, 1, 5),
            at(6, feat, 0, 5),
        ],
    )

    lanes_total = None
    for k in range(layers - 1):
        grid = gw[k]
        folded = jnp.zeros((width, tall), F32)
        for a in range(each):
            folded = folded + jnp.where(
                lane // width == a, grid[a * width : (a + 1) * width], 0.0
            )
        folded = jnp.concatenate([folded, grid[tall : tall + 8]], axis=0)
        src, dst = iota((tall, 128), 0), iota((tall, 128), 1)
        fold = (lax.rem(src, width) + k * width == dst).astype(BF16)
        pieces = contract(split3(folded), fold, 1, 0)
        size = width + 8
        piece = pieces[:size] + pieces[size : 2 * size] + pieces[2 * size :]
        lanes_total = piece if lanes_total is None else lanes_total + piece
    end_sum.start(0, lanes_total)
    feat(1, 6)
    feat(0, 6)
    end_sum.middle(0)
    gtail_ref[...] = end_sum.finish(0)


def ends_kernel(
    dims,
    one_ref,
    feat_all,
    means,
    pre_all,
    tail,
    oneout_ref,
    gself_ref,
    gmeans_ref,
    grows_ref,
    gcols_ref,
    gbias_ref,
    gwpair_ref,
    gbpair_ref,
    gself,
    gmeans,
    grows,
    gcols,
    gbias,
    gwpair,
    gbpair,
    sem,
):
    walkers, width, one_width, layers, far = dims
    blocks = 4 * far
    rows = feat_all.shape[-2]
    edges = [0, one_width, one_width + 2 * width, one_width + 4 * width]
    moves = []

    def move(src, dst):
        copy = pltpu.make_async_copy(src, dst, sem.at[len(moves)])
        copy.start()
        moves.append(copy)

    move(one_ref, oneout_ref)
    for layer in range(layers):
        for b in range(blocks):
            for n, out in enumerate((gself, grows, gcols)):
                low, high = max(edges[n], b * rows), min(edges[n + 1], (b + 1) * rows)
                if low < high:
                    out[layer, low - edges[n] : high - edges[n]] = feat_all[
                        layer, b // 4, (b // 2) % 2, b % 2, low - b * rows : high - b * rows
                    ]
        move(gself.at[layer], gself_ref.at[layer])
    move(grows, grows_ref)
    move(gcols, gcols_ref)
    for layer in range(layers):
        total = pre_all[layer]
        pieces = split3(total)
        mean = means[layer].astype(F32)
        for s in range(2):
            piece = mean[s * walkers : (s + 1) * walkers]
            tripled = jnp.concatenate([piece, piece, piece], axis=0).astype(BF16)
            gmeans[layer, s * one_width : (s + 1) * one_width] = contract(tripled, pieces, 0, 0)
        move(gmeans.at[layer], gmeans_ref.at[layer])
        gbias[layer : layer + 1] = jnp.sum(total, axis=0, keepdims=True)
    for k in range(layers - 1):
        gwpair[k] = tail[:width, k * width : (k + 1) * width]
        gbpair[k : k + 1] = tail[width : width + 1, k * width : (k + 1) * width]
    move(gbias, gbias_ref)
    move(gwpair, gwpair_ref)
    move(gbpair, gbpair_ref)
    for copy in moves:
        copy.wait()


def local(
    size,
    one_input,
    pair_input,
    spins,
    cotangent,
    w_self,
    w_means,
    w_rows,
    w_cols,
    b_one,
    w_pair,
    b_pair,
):
    walkers, rows, one_width = one_input.shape
    width, electrons = pair_input.shape[2:]
    layers = w_self.shape[0]
    far = size // 4
    if rows * width != 1024 or width != 32 or walkers != 8 or layers != 3 or far < 2:
        return general(
            size,
            one_input,
            pair_input,
            spins,
            cotangent,
            w_self,
            w_means,
            w_rows,
            w_cols,
            b_one,
            w_pair,
            b_pair,
        )
    flat = walkers * rows
    tall_all = rows * width
    tall = 8 * width
    pairs = walkers // 2
    parts = layers * pairs
    deep = one_width + 4 * width
    block = deep // size
    lanes = 4 * width
    dims = (walkers, rows, width, electrons, one_width, layers, far, tall)
    vmem = pltpu.VMEM
    scratch = [
        vmem((walkers, tall_all, electrons), BF16),
        vmem((walkers, tall_all, electrons), BF16),
        vmem((walkers, tall_all, electrons), BF16),
        vmem((walkers, tall_all, electrons), BF16),
        vmem((walkers, 16, electrons), BF16),
        vmem((walkers, 2 * width, tall_all), BF16),
        vmem((layers - 1, tall, tall), BF16),
        vmem((layers - 1, tall, tall), BF16),
        vmem((layers - 1, tall, 1), F32),
        vmem((layers, one_width + 2 * lanes, one_width), BF16),
        vmem((2 * walkers, flat), BF16),
        vmem((flat, one_width), F32),
        vmem((2, flat, 2 * lanes), F32),
        vmem((walkers, rows, lanes), F32),
        vmem((walkers, 8, 2 * lanes), F32),
        vmem((layers, walkers, 8, 2 * lanes), F32),
        vmem((layers, flat, one_width + 2 * lanes), BF16),
        vmem((layers, flat, one_width), F32),
        vmem((flat, one_width), F32),
        vmem((2, 2 * width, electrons), F32),
        vmem((2, 2 * lanes, electrons), BF16),
        vmem((2, tall + 16, tall), F32),
        vmem((parts, far, 2, 2, rows, lanes), F32),
        vmem((parts, far, 2, rows, lanes), F32),
        vmem((parts, far, rows, lanes), F32),
        vmem((parts, far - 1, rows, lanes), F32),
        vmem((parts, rows, lanes), F32),
        vmem((2, far, 2, 2, pairs, rows, lanes), F32),
        vmem((layers, far, 2 * walkers, one_width), F32),
        vmem((layers, 4, 2 * walkers, one_width), F32),
        vmem((layers, far, walkers, one_width), F32),
        vmem((layers, 4, walkers, one_width), F32),
        vmem((1, far, width + 8, 128), F32),
        vmem((1, 4, width + 8, 128), F32),
        vmem((layers, far, 2, 2, block, one_width), F32),
        vmem((layers, far, 2, block, one_width), F32),
        vmem((layers, far, block, one_width), F32),
        vmem((layers, far, block, one_width), F32),
    ]
    scratch += dma((walkers,), (walkers,))
    scratch += dma((parts,), (parts,), (parts,), (parts,), (parts, far), (parts, far))
    scratch += dma((2, far), (2, far), (2, far), (2, far), (2,), (2,))
    scratch += dma(*([(layers, far), (layers, far), (layers, 4), (layers, 4)] * 2))
    scratch += dma((1, far), (1, far), (1, 4), (1, 4))
    scratch += dma(*[(layers, n) for n in (1, 1, 1, 1, far, far, far, far, 1, 1, 1, 1)])
    in_vmem = pl.BlockSpec(memory_space=pltpu.VMEM)
    shape = jax.ShapeDtypeStruct
    out = pl.pallas_call(
        functools.partial(whole_kernel, dims),
        out_shape=(
            shape((flat, one_width), BF16),
            shape((layers, far, 2, 2, block, one_width), F32),
            shape((layers, 2 * walkers, one_width), BF16),
            shape((layers, walkers, one_width), F32),
            shape((width + 8, 128), F32),
        ),
        in_specs=[in_vmem, pl.BlockSpec(memory_space=pl.ANY)] + [in_vmem] * 9,
        out_specs=(in_vmem,) * 5,
        scratch_shapes=scratch,
        compiler_params=pltpu.CompilerParams(
            vmem_limit_bytes=60 * 1024 * 1024, collective_id=0, has_side_effects=True
        ),
    )(
        one_input.reshape(flat, one_width),
        pair_input.reshape(walkers, tall_all, electrons),
        spins,
        cotangent.reshape(flat, one_width),
        w_self,
        w_means,
        w_rows,
        w_cols,
        b_one,
        w_pair,
        b_pair,
    )
    results = (
        shape((flat, one_width), BF16),
        shape((layers, one_width, one_width), F32),
        shape((layers, 2 * one_width, one_width), F32),
        shape((layers, 2 * width, one_width), F32),
        shape((layers, 2 * width, one_width), F32),
        shape((layers, one_width), F32),
        shape((layers - 1, width, width), F32),
        shape((layers - 1, width), F32),
    )
    anywhere = pl.BlockSpec(memory_space=pl.ANY)
    one_out, *rest = pl.pallas_call(
        functools.partial(ends_kernel, (walkers, width, one_width, layers, far)),
        out_shape=results,
        in_specs=[in_vmem] * 5,
        out_specs=(anywhere,) * len(results),
        scratch_shapes=[vmem(results[n].shape, F32) for n in range(1, 8)]
        + dma((2 * layers + 6,)),
    )(*out)
    return one_out.reshape(walkers, rows, one_width), *rest


def solution(mesh):
    in_specs = (
        P("group", "row", None),
        P("group", "row", None, None),
        P("group", None),
        P("group", "row", None),
        P(),
        P(),
        P(),
        P(),
        P(),
        P(),
        P(),
    )
    out_specs = (
        P("group", "row", None),
        P("group", None, None),
        P("group", None, None),
        P("group", None, None),
        P("group", None, None),
        P("group", None),
        P("group", None, None),
        P("group", None),
    )
    return jax.shard_map(
        functools.partial(local, mesh.shape["row"]),
        mesh=mesh,
        in_specs=in_specs,
        out_specs=out_specs,
        check_vma=False,
    )
```
